256 devices in a mesh: space: 32 (over x_lo, z, core), src: 8 (over y, x_hi).
Axes of the slice: x: 4 (x_hi: 2, x_lo: 2; x = x_hi * 2 + x_lo), y: 4, z: 8, core: 2. Of those that a mesh axis runs over, the one named last changes fastest.
Arguments:
- medium: float32 [32, 64, 64, 64], P('space'), may hold values from 0.8 to 1.2
- source_cells: int32 [8, 4096], P('src'), may hold values from 0 to 8388607, as said below
- source_weights: float32 [2, 8, 4096], P(None, 'src'), may hold values from -48 to 48
- adjoint: bfloat16 [2, 8, 32, 64, 64, 64], P(None, 'src', 'space'), may hold values from -6 to 6
Outputs:
- field: float32 [2, 8, 32, 64, 64, 64], P(None, 'src', 'space')
- gradient: float32 [32, 64, 64, 64], P('space', 'src')
The draws below stay inside these ranges and needn't reach their ends.
Inputs may be any that keep to these rules, and one draw needn't show every extreme that they name: source_cells[s, p] is the cell b * 64**3 + (x * 64 + y) * 64 + z of the point p of source s; points may repeat and fall in any box.
All inputs are finite; a program needn't handle non-finite values.
Results may differ from the reference program's by a relative error of at most 0.0003.
Values sent between devices are 32-bit elements; how exact they have to be, the bound alone decides.
A program may use at most 128 MiB of HBM per device.

```python
import jax
import jax.numpy as jnp
from jax import lax

BOX = 64
TERMS = 2
BGX = 2
BGZ = 4
BGY = 4
BOXES = 32
SOURCES = 8
PTS = 4096
CELLS = 8388608


def draw_source_cells(key, part):
    values = jax.random.randint(key, (SOURCES, PTS), 0, CELLS, dtype=jnp.int32)
    values = values.at[0, 0].set(0)
    values = values.at[0, 1].set(CELLS - 1)
    return values


def block_levels(stream_key, shape, pieces, least, largest):
    factor_of, own = 1.0, jax.random.fold_in(stream_key, 6)
    for dim, shards_of in pieces:
        draws = jnp.exp(jax.random.uniform(jax.random.fold_in(own, dim), (shards_of,), jnp.float32, least / len(pieces), largest / len(pieces)))
        factor_of = factor_of * jnp.repeat(draws, shape[dim] // shards_of).reshape([-1 if axis == dim else 1 for axis in range(len(shape))])
    return factor_of


def centred(own_key, extent, scale, limit, pieces=(), held_as=jnp.bfloat16):
    level = block_levels(own_key, extent, pieces, -0.22, 0.18) if pieces else 1.0
    array = jax.random.normal(own_key, extent, jnp.float32) * scale * level
    return jnp.minimum(jnp.maximum(array, -limit), limit).astype(held_as)


def setup_inputs(seed: int = 0) -> dict:
    keys = jax.random.split(jax.random.key(seed), 5)
    medium = jnp.clip(0.8 + 0.40000004 * jax.random.uniform(keys[0], (BOXES, BOX, BOX, BOX), jnp.float32) ** block_levels(keys[0], (BOXES, BOX, BOX, BOX), ((0, 32),), -0.2, 0.2), 0.8, 1.2)
    source_cells = draw_source_cells(jax.random.fold_in(keys[4], 71), 0)
    source_weights = centred(keys[2], (2, SOURCES, PTS), 8.0, 48.0, ((1, 8),), jnp.float32)
    adjoint = centred(keys[3], (2, SOURCES, BOXES, BOX, BOX, BOX), 1.0, 6.0, ((1, 8), (2, 32)))
    return dict(medium=medium, source_cells=source_cells, source_weights=source_weights, adjoint=adjoint)


wave_sq = 1.0
damping = 0.25


def green_kernel():
    frequency = jnp.arange(BOX, dtype=jnp.float32)
    eigenvalue = 2.0 - 2.0 * jnp.cos((2.0 * jnp.pi / BOX) * frequency)
    summed = eigenvalue[:, None, None] + eigenvalue[None, :, None] + eigenvalue[None, None, :]
    shifted = summed - wave_sq
    denominator = shifted * shifted + damping * damping
    return shifted / denominator, damping / denominator


def green(real_part, imag_part, kernel):
    spectrum = jnp.fft.fftn(real_part + 1j * imag_part, axes=(1, 2, 3))
    result = jnp.fft.ifftn(spectrum * (kernel[0] + 1j * kernel[1]), axes=(1, 2, 3))
    return jnp.real(result), jnp.imag(result)


def to_grid(values):
    blocks = values.reshape(BGX, BGY, BGZ, BOX, BOX, BOX)
    return blocks.transpose(0, 3, 1, 4, 2, 5).reshape(BGX * BOX, BGY * BOX, BGZ * BOX)


def to_boxes(values):
    blocks = values.reshape(BGX, BOX, BGY, BOX, BGZ, BOX)
    return blocks.transpose(0, 2, 4, 1, 3, 5).reshape(BOXES, BOX, BOX, BOX)


def correction(values):
    padded = jnp.pad(to_grid(values), 1)
    global_sum = padded[2:, 1:-1, 1:-1] + padded[:-2, 1:-1, 1:-1]
    global_sum = global_sum + padded[1:-1, 2:, 1:-1] + padded[1:-1, :-2, 1:-1]
    global_sum = global_sum + padded[1:-1, 1:-1, 2:] + padded[1:-1, 1:-1, :-2]
    local_sum = jnp.roll(values, -1, 1) + jnp.roll(values, 1, 1)
    local_sum = local_sum + jnp.roll(values, -1, 2) + jnp.roll(values, 1, 2)
    local_sum = local_sum + jnp.roll(values, -1, 3) + jnp.roll(values, 1, 3)
    return to_boxes(global_sum) - local_sum


def reference(medium, source_cells, source_weights, adjoint):
    kernel = green_kernel()
    potential = medium - wave_sq
    ratio = potential / damping
    cube = BOX ** 3

    def one_source(inputs):
        cells, weights_real, weights_imag = inputs
        source_real = jax.ops.segment_sum(weights_real, cells, num_segments=BOXES * cube).reshape(BOXES, BOX, BOX, BOX)
        source_imag = jax.ops.segment_sum(weights_imag, cells, num_segments=BOXES * cube).reshape(BOXES, BOX, BOX, BOX)
        green_real, green_imag = green(source_real, source_imag, kernel)
        field_real = green_real - ratio * green_imag
        field_imag = green_imag + ratio * green_real
        for term_index in range(TERMS):
            drive_real = potential * field_real + damping * field_imag + source_real + correction(field_real)
            drive_imag = potential * field_imag - damping * field_real + source_imag + correction(field_imag)
            green_real, green_imag = green(drive_real, drive_imag, kernel)
            update_real = field_real - green_real
            update_imag = field_imag - green_imag
            field_real = field_real - (update_real - ratio * update_imag)
            field_imag = field_imag - (update_imag + ratio * update_real)
        return jnp.stack([field_real, field_imag])

    fields = lax.map(one_source, (source_cells, source_weights[0], source_weights[1]))
    field = jnp.swapaxes(fields, 0, 1)
    adjoint_full = adjoint.astype(jnp.float32)
    gradient = jnp.sum(adjoint_full[0] * field[0] - adjoint_full[1] * field[1], axis=0)
    return field, gradient
```

```python
import functools

import jax
import jax.numpy as jnp
import numpy as np
from jax import lax
from jax.experimental import pallas as pl
from jax.experimental.pallas import tpu as pltpu
from jax.sharding import PartitionSpec as P

N = 64
ROWS = N * N
LANES = 2 * N
TERMS = 2
BGX, BGY, BGZ = 2, 4, 4
SRC = 8
SLAB = N // SRC
CH = SLAB * N
DAMP = 0.25
MESH = pl.DeviceIdType.MESH
SLOTS = 256
F32, BF16 = jnp.float32, jnp.bfloat16


def split(values):
    high = values.astype(BF16)
    low = (values - high.astype(F32)).astype(BF16)
    return high, low


def dft_table(sign):
    k = np.arange(N)
    phase = 2.0 * np.pi / N * (k[:, None] * k[None, :] % N)
    c, s = np.cos(phase), sign * np.sin(phase)
    w = np.block([[c, s], [-s, c]]).astype(np.float32)
    high = w.astype(BF16)
    low = (w - high.astype(np.float32)).astype(BF16)
    half = np.concatenate([high, low], axis=1)
    return np.concatenate([half, half], axis=0)


def along_lanes(values, table):
    high, low = split(values)
    out = jnp.dot(jnp.concatenate([high, low], axis=1), table, preferred_element_type=F32)
    return out[:, :LANES] + out[:, LANES:]


def swapped(values):
    lower = lax.broadcasted_iota(jnp.int32, (N, LANES), 1) < N
    blocks = []
    for start in range(0, values.shape[0], LANES):
        turned = values[start : start + LANES].T
        re, im = turned[:N], turned[N:]
        blocks.append(jnp.where(lower, re, pltpu.roll(im, N, 1)))
        blocks.append(jnp.where(lower, pltpu.roll(re, N, 1), im))
    return jnp.concatenate(blocks, axis=0)


def place_kernel(box_ref, cells_ref, wre_ref, wim_ref, out_ref, pos_ref, feat_ref):
    cells = cells_ref[...] - box_ref[0] * (N * N * N)
    inside = (cells >= 0) & (cells < N * N * N)
    mask = jnp.where(inside, 1.0, 0.0).astype(BF16)
    groups = cells.shape[0]
    i0 = lax.broadcasted_iota(jnp.int32, (128, 128), 0)
    i1 = lax.broadcasted_iota(jnp.int32, (128, 128), 1)
    upper = jnp.where(i0 < i1, 1.0, 0.0).astype(BF16)
    within = jnp.dot(mask, upper, preferred_element_type=F32)
    totals = jnp.dot(mask, jnp.ones((128, 128), BF16), preferred_element_type=F32)
    j0 = lax.broadcasted_iota(jnp.int32, (groups, groups), 0)
    j1 = lax.broadcasted_iota(jnp.int32, (groups, groups), 1)
    before = jnp.where(j1 < j0, 1.0, 0.0).astype(BF16)
    offset = jnp.dot(before, totals.astype(BF16), preferred_element_type=F32)
    pos_ref[...] = jnp.where(inside, (within + offset).astype(jnp.int32), -1)
    count = jnp.sum(jnp.where(inside, 1, 0))
    safe = jnp.where(inside, cells, 0)
    rh, rl = split(wre_ref[...])
    ih, il = split(wim_ref[...])
    rows = (
        (safe // ROWS).astype(F32),
        (safe // N % N).astype(F32),
        (safe % N).astype(F32),
        rh.astype(F32),
        rl.astype(F32),
        ih.astype(F32),
        il.astype(F32),
    )
    for n, row in enumerate(rows):
        feat_ref[n] = row

    def chunk(step, carry):
        slot = lax.broadcasted_iota(jnp.int32, (SLOTS, 128), 0) + step * SLOTS
        sub = lax.broadcasted_iota(jnp.int32, (16, 128), 0)
        hots, feats = [], []
        for g in range(groups):
            hots.append(jnp.where(pos_ref[g : g + 1, :] == slot, 1.0, 0.0).astype(BF16))
            f = jnp.zeros((16, 128), F32)
            for n in range(len(rows)):
                f = jnp.where(sub == n, feat_ref[n, g : g + 1, :], f)
            feats.append(f.astype(BF16))
        hot = jnp.concatenate(hots, axis=1)
        feat = jnp.concatenate(feats, axis=1)
        nt = (((1,), (1,)), ((), ()))
        by_lane = lax.dot_general(feat, hot, nt, preferred_element_type=F32)
        by_row = lax.dot_general(hot, feat, nt, preferred_element_type=F32)
        used = lax.broadcasted_iota(jnp.int32, (1, SLOTS), 1) + step * SLOTS < count
        plane = (by_lane[0:1] * N + by_lane[1:2]).astype(jnp.int32)
        plane = jnp.where(used, plane, -1)
        lane = lax.broadcasted_iota(jnp.int32, (SLOTS, LANES), 1)
        hit = lane % N == by_row[:, 2:3].astype(jnp.int32)
        first = lane < N
        high = jnp.where(hit, jnp.where(first, by_row[:, 3:4], by_row[:, 5:6]), 0.0)
        low = jnp.where(hit, jnp.where(first, by_row[:, 4:5], by_row[:, 6:7]), 0.0)
        spread = jnp.concatenate([high, low], axis=1).astype(BF16)

        def rows_of(block, inner):
            start = pl.multiple_of(block * 512, 512)
            at = lax.broadcasted_iota(jnp.int32, (512, SLOTS), 0) + start
            pick = jnp.where(at == plane, 1.0, 0.0).astype(BF16)
            got = jnp.dot(pick, spread, preferred_element_type=F32)
            got = got[:, :LANES] + got[:, LANES:]
            old = out_ref[pl.ds(start, 512), :]
            out_ref[pl.ds(start, 512), :] = jnp.where(step > 0, old, 0.0) + got
            return inner

        return lax.fori_loop(0, ROWS // 512, rows_of, carry)

    lax.fori_loop(0, jnp.maximum(1, (count + SLOTS - 1) // SLOTS), chunk, 0)


def place(box, cells, weights):
    groups = cells.shape[-1] // 128
    return pl.pallas_call(
        place_kernel,
        out_shape=jax.ShapeDtypeStruct((ROWS, LANES), F32),
        in_specs=[pl.BlockSpec(memory_space=pltpu.SMEM)]
        + [pl.BlockSpec(memory_space=pltpu.VMEM)] * 3,
        out_specs=pl.BlockSpec(memory_space=pltpu.VMEM),
        scratch_shapes=[pltpu.VMEM((groups, 128), jnp.int32), pltpu.VMEM((8, groups, 128), F32)],
    )(
        box,
        cells.reshape(groups, 128),
        weights[0].reshape(groups, 128),
        weights[1].reshape(groups, 128),
    )


def series_kernel(
    remote,
    eig_ref, pair_ref, fwd_ref, inv_ref, medium_ref, source_ref, adjoint_ref,
    out_ref, grad_ref,
    field, drive, one, two, kre, kim, faces, zcor, recv, gsend, grecv,
    send_sem, recv_sem, gsend_sem, grecv_sem, out_sem,
):
    if remote:
        space, me = lax.axis_index("space"), lax.axis_index("src")
        bx, by, bz = space // (BGY * BGZ), space // BGZ % BGY, space % BGZ
        below = (
            lax.rem(bx + BGX - 1, BGX) * (BGY * BGZ) + by * BGZ + bz,
            bx * (BGY * BGZ) + lax.rem(by + BGY - 1, BGY) * BGZ + bz,
            bx * (BGY * BGZ) + by * BGZ + lax.rem(bz + BGZ - 1, BGZ),
        )
        above = (
            lax.rem(bx + 1, BGX) * (BGY * BGZ) + by * BGZ + bz,
            bx * (BGY * BGZ) + lax.rem(by + 1, BGY) * BGZ + bz,
            bx * (BGY * BGZ) + by * BGZ + lax.rem(bz + 1, BGZ),
        )
        has_below = [(v > 0).astype(F32) for v in (bx, by, bz)]
        has_above = [(v < e - 1).astype(F32) for v, e in ((bx, BGX), (by, BGY), (bz, BGZ))]
        barrier = pltpu.get_barrier_semaphore()
        for d in range(3):
            for other in (below[d], above[d]):
                pl.semaphore_signal(barrier, 1, device_id={"space": other}, device_id_type=MESH)
        for k in range(1, SRC):
            pl.semaphore_signal(
                barrier, 1, device_id={"src": lax.rem(me + k, SRC)}, device_id_type=MESH
            )
    else:
        me = 0

    wide = lax.broadcasted_iota(jnp.int32, (CH, LANES), 1) < N
    lower = lax.broadcasted_iota(jnp.int32, (N, LANES), 1) < N

    def table(z, carry):
        rows = pl.ds(pl.multiple_of(z * N, N), N)
        shifted = pair_ref[...] + eig_ref[z]
        scale = 1.0 / ((shifted * shifted + DAMP * DAMP) * float(N**3))
        kre[rows, :] = shifted * scale
        kim[rows, :] = jnp.where(lower, -DAMP, DAMP) * scale
        return carry

    lax.fori_loop(0, N, table, 0)
    field[...] = jnp.zeros_like(field)
    zcor[...] = jnp.zeros_like(zcor)

    if remote:
        pl.semaphore_wait(barrier, 6 + SRC - 1)

    def chunk_rows(i):
        return pl.ds(pl.multiple_of(i * CH, CH), CH)

    def forward(origin):
        def z_pass(i, carry):
            rows = chunk_rows(i)
            values = origin[rows, :]
            at = lax.broadcasted_iota(jnp.int32, (LANES, LANES), 0)
            extra = []
            for p in range(SLAB // 2):
                pair = i * (SLAB // 2) + p
                block = jnp.zeros((LANES, LANES), F32)
                for face in range(2):
                    for part in range(2):
                        line = zcor[face, pl.ds(part * (N // 2) + pair, 1), :]
                        block = jnp.where(at == part * N + face * (N - 1), line, block)
                extra.append(block.T)
            values = values + jnp.concatenate(extra, axis=0)
            one[rows, :] = swapped(along_lanes(values, fwd_ref[...]))
            return carry

        lax.fori_loop(0, SRC, z_pass, 0)

    def middle():
        def xy_pass(i, carry):
            rows = chunk_rows(i)
            parts = [one[pl.ds(i * SLAB + z, N, stride=N), :] for z in range(SLAB)]
            values = along_lanes(jnp.concatenate(parts, axis=0), fwd_ref[...])
            values = along_lanes(swapped(values), fwd_ref[...])
            values = kre[rows, :] * values + kim[rows, :] * pltpu.roll(values, N, 1)
            values = swapped(along_lanes(values, inv_ref[...]))
            values = along_lanes(values, inv_ref[...])
            for z in range(SLAB):
                two[pl.ds(i * SLAB + z, N, stride=N), :] = values[z * N : (z + 1) * N]
            return carry

        lax.fori_loop(0, SRC, xy_pass, 0)

    def updated(rows):
        green = along_lanes(swapped(two[rows, :]), inv_ref[...])
        plain = medium_ref[rows, :] - 1.0
        potential = jnp.concatenate([plain, plain], axis=1)
        ratio = jnp.where(wide, -1.0 / DAMP, 1.0 / DAMP) * potential
        new = green - ratio * pltpu.roll(field[rows, :] - green, N, 1)
        return new, potential

    def term(step, carry):
        forward(drive)
        middle()

        def z_pass(i, inner):
            rows = chunk_rows(i)
            new, potential = updated(rows)
            field[rows, :] = new
            turn = jnp.where(wide, DAMP, -DAMP) * pltpu.roll(new, N, 1)
            drive[rows, :] = potential * new + turn + source_ref[rows, :]
            for p in range(SLAB // 2):
                pair = i * (SLAB // 2) + p
                block = new[p * LANES : (p + 1) * LANES].T
                for face in range(2):
                    for part in range(2):
                        line = part * N + face * (N - 1)
                        faces[2 + face, pl.ds(part * (N // 2) + pair, 1), :] = block[line : line + 1]
            return inner

        lax.fori_loop(0, SRC, z_pass, 0)
        first, last = pl.ds(0, N), pl.ds(ROWS - N, N)
        y_first, y_last = pl.ds(0, N, stride=N), pl.ds(N - 1, N, stride=N)
        faces[0] = field[y_first, :]
        faces[1] = field[y_last, :]
        if remote:
            sends = (
                (field.at[first], field.at[last]),
                (faces.at[0], faces.at[1]),
                (faces.at[2], faces.at[3]),
            )
            copies = []
            for d in range(3):
                for side, other in ((1, above[d]), (0, below[d])):
                    slot = 2 * d + 1 - side
                    copies.append(
                        pltpu.make_async_remote_copy(
                            src_ref=sends[d][side],
                            dst_ref=recv.at[step, slot],
                            send_sem=send_sem.at[step, slot],
                            recv_sem=recv_sem.at[step, slot],
                            device_id={"space": other},
                            device_id_type=MESH,
                        )
                    )
            for copy in copies:
                copy.start()
            for copy in copies:
                copy.wait()
            got = [[m * recv[step, 2 * d + s] for s, m in ((0, has_below[d]), (1, has_above[d]))] for d in range(3)]
        else:
            got = [[0.0, 0.0]] * 3
        drive[first, :] = drive[first, :] + (got[0][0] - field[last, :])
        drive[last, :] = drive[last, :] + (got[0][1] - field[first, :])
        drive[y_first, :] = drive[y_first, :] + (got[1][0] - faces[1])
        drive[y_last, :] = drive[y_last, :] + (got[1][1] - faces[0])
        zcor[0] = got[2][0] - faces[3]
        zcor[1] = got[2][1] - faces[2]
        return carry

    drive[...] = source_ref[...]
    lax.fori_loop(0, TERMS, term, 0)

    forward(drive)
    middle()

    def grad_copy(owner, slot):
        return pltpu.make_async_remote_copy(
            src_ref=gsend.at[owner],
            dst_ref=grecv.at[slot],
            send_sem=gsend_sem.at[owner],
            recv_sem=grecv_sem.at[slot],
            device_id={"src": owner},
            device_id_type=MESH,
        )

    def out_copy(i):
        rows = chunk_rows(i)
        return pltpu.make_async_copy(field.at[rows], out_ref.at[rows], out_sem.at[i])

    def last_pass(k, carry):
        i = lax.rem(me + 1 + k, SRC)
        rows = chunk_rows(i)
        new, _ = updated(rows)
        field[rows, :] = new
        out_copy(i).start()
        both = jnp.concatenate([adjoint_ref[0, rows, :], adjoint_ref[1, rows, :]], axis=1)
        terms = both.astype(F32) * new
        terms = terms - pltpu.roll(terms, N, 1)
        half = CH // 2
        gsend[i] = jnp.where(wide[:half], terms[:half], -terms[half:])
        if remote:

            @pl.when(k < SRC - 1)
            def _():
                grad_copy(i, me).start()

        return carry

    lax.fori_loop(0, SRC, last_pass, 0)
    total = gsend[me]
    if remote:
        for k in range(1, SRC):
            other = lax.rem(me + k, SRC)
            grad_copy(other, other).wait_recv()
            total = total + grecv[other]
    grad_ref[0 : CH // 2, :] = total[:, :N]
    grad_ref[CH // 2 :, :] = pltpu.roll(total, N, 1)[:, :N]
    if remote:
        for k in range(1, SRC):
            grad_copy(lax.rem(me + k, SRC), me).wait_send()
    for i in range(SRC):
        out_copy(i).wait()


def series(medium, source, adjoint, remote=True):
    eig = 2.0 - 2.0 * np.cos(2.0 * np.pi / N * np.arange(N))
    both = np.concatenate([eig, eig])
    pair = (eig[:, None] + both[None, :] - 1.0).astype(np.float32)
    big = lambda: pltpu.VMEM((ROWS, LANES), F32)
    face = (N, LANES)
    vmem = pl.BlockSpec(memory_space=pltpu.VMEM)
    return pl.pallas_call(
        functools.partial(series_kernel, remote),
        out_shape=(
            jax.ShapeDtypeStruct((ROWS, LANES), F32),
            jax.ShapeDtypeStruct((CH, N), F32),
        ),
        in_specs=[pl.BlockSpec(memory_space=pltpu.SMEM)] + [vmem] * 6,
        out_specs=(pl.BlockSpec(memory_space=pl.ANY), vmem),
        scratch_shapes=[
            big(), big(), big(), big(), big(), big(),
            pltpu.VMEM((4,) + face, F32),
            pltpu.VMEM((2,) + face, F32),
            pltpu.VMEM((TERMS, 6) + face, F32),
            pltpu.VMEM((SRC, CH // 2, LANES), F32),
            pltpu.VMEM((SRC, CH // 2, LANES), F32),
            pltpu.SemaphoreType.DMA((TERMS, 6)),
            pltpu.SemaphoreType.DMA((TERMS, 6)),
            pltpu.SemaphoreType.DMA((SRC,)),
            pltpu.SemaphoreType.DMA((SRC,)),
            pltpu.SemaphoreType.DMA((SRC,)),
        ],
        compiler_params=pltpu.CompilerParams(
            collective_id=0 if remote else None,
            has_side_effects=remote,
            vmem_limit_bytes=60 * 1024 * 1024,
        ),
    )(
        jnp.asarray(eig.astype(np.float32)),
        jnp.asarray(pair),
        jnp.asarray(dft_table(-1.0)),
        jnp.asarray(dft_table(1.0)),
        medium.reshape(ROWS, N),
        source,
        adjoint.reshape(2, ROWS, N),
    )


def local(medium, source_cells, source_weights, adjoint):
    box = lax.axis_index("space").astype(jnp.int32).reshape(1)
    source = place(box, source_cells, source_weights)
    packed, owned = series(medium, source, adjoint)
    field = packed.reshape(N, N, 2, N).transpose(2, 0, 1, 3)
    return field[:, None, None], owned.reshape(1, SLAB, N, N)


def solution(mesh):
    placed = (
        P("space", None, None, None),
        P("src", None),
        P(None, "src", None),
        P(None, "src", "space", None, None, None),
    )
    return jax.shard_map(
        local,
        mesh=mesh,
        in_specs=placed,
        out_specs=(P(None, "src", "space", None, None, None), P("space", "src", None, None)),
        check_vma=False,
    )
```

```python
import functools

import jax
import jax.numpy as jnp
import numpy as np
from jax import lax
from jax.experimental import pallas as pl
from jax.experimental.pallas import tpu as pltpu
from jax.sharding import PartitionSpec as P

N = 64
ROWS = N * N
LANES = 2 * N
TERMS = 2
BGX, BGY, BGZ = 2, 4, 4
SRC = 8
SLAB = N // SRC
CH = SLAB * N
DAMP = 0.25
PITCH = 72
BACK, BACKS = 256, 4
ITEM = 512
MESH = pl.DeviceIdType.MESH
SLOTS = 256
F32, BF16 = jnp.float32, jnp.bfloat16


def split(values):
    high = values.astype(BF16)
    low = (values - high.astype(F32)).astype(BF16)
    return high, low


def dft_table(sign):
    k = np.arange(N)
    phase = 2.0 * np.pi / N * (k[:, None] * k[None, :] % N)
    c, s = np.cos(phase), sign * np.sin(phase)
    w = np.block([[c, s], [-s, c]]).astype(np.float32)
    high = w.astype(BF16)
    low = (w - high.astype(np.float32)).astype(BF16)
    half = np.concatenate([high, low], axis=1)
    return np.concatenate([half, half], axis=0)


def along_lanes(values, table):
    high, low = split(values)
    out = jnp.dot(jnp.concatenate([high, low], axis=1), table, preferred_element_type=F32)
    return out[:, :LANES] + out[:, LANES:]


def lower_half(rows):
    return lax.broadcasted_iota(jnp.int32, (rows, LANES), 1) < N


def trade(first, second):
    lower = lower_half(first.shape[0])
    crossed = pltpu.roll(jnp.where(lower, second, first), N, 1)
    return jnp.where(lower, first, crossed), jnp.where(lower, crossed, second)


def swapped(values, exchange=False):
    blocks = []
    for start in range(0, values.shape[0], LANES):
        turned = values[start : start + LANES].T
        first, second = turned[:N], turned[N:]
        blocks += trade(second, first) if exchange else trade(first, second)
    return jnp.concatenate(blocks, axis=0)


def staggered(count, stages):
    held = {}
    for turn in range(count + len(stages) - 1):
        for n in reversed(range(len(stages))):
            item = turn - n
            if 0 <= item < count:
                held[item] = stages[n](item, held.get(item))


def place_kernel(box_ref, cells_ref, weights_ref, out_ref, pos_ref, feat_ref):
    cells = cells_ref[...] - box_ref[0] * (N * N * N)
    inside = (cells >= 0) & (cells < N * N * N)
    mask = jnp.where(inside, 1.0, 0.0).astype(BF16)
    groups = cells.shape[0]
    i0 = lax.broadcasted_iota(jnp.int32, (128, 128), 0)
    i1 = lax.broadcasted_iota(jnp.int32, (128, 128), 1)
    upper = jnp.where(i0 < i1, 1.0, 0.0).astype(BF16)
    within = jnp.dot(mask, upper, preferred_element_type=F32)
    totals = jnp.dot(mask, jnp.ones((128, 128), BF16), preferred_element_type=F32)
    j0 = lax.broadcasted_iota(jnp.int32, (groups, groups), 0)
    j1 = lax.broadcasted_iota(jnp.int32, (groups, groups), 1)
    before = jnp.where(j1 < j0, 1.0, 0.0).astype(BF16)
    offset = jnp.dot(before, totals.astype(BF16), preferred_element_type=F32)
    pos_ref[...] = jnp.where(inside, (within + offset).astype(jnp.int32), -1)
    count = jnp.sum(jnp.where(inside, 1, 0))
    safe = jnp.where(inside, cells, 0)
    rh, rl = split(weights_ref[0])
    ih, il = split(weights_ref[1])
    rows = (
        (safe >> 13).astype(F32),
        ((safe >> 6) & (N - 1)).astype(F32),
        (((safe >> 12) & 1) * N + (safe & (N - 1))).astype(F32),
        rh.astype(F32),
        rl.astype(F32),
        ih.astype(F32),
        il.astype(F32),
    )
    for n, row in enumerate(rows):
        feat_ref[n] = row

    def chunk(step, carry):
        slot = lax.broadcasted_iota(jnp.int32, (SLOTS, 128), 0) + step * SLOTS
        sub = lax.broadcasted_iota(jnp.int32, (16, 128), 0)
        hots, feats = [], []
        for g in range(groups):
            hots.append(jnp.where(pos_ref[g : g + 1, :] == slot, 1.0, 0.0).astype(BF16))
            f = jnp.zeros((16, 128), F32)
            for n in range(len(rows)):
                f = jnp.where(sub == n, feat_ref[n, g : g + 1, :], f)
            feats.append(f.astype(BF16))
        hot = jnp.concatenate(hots, axis=1)
        feat = jnp.concatenate(feats, axis=1)
        nt = (((1,), (1,)), ((), ()))
        by_lane = lax.dot_general(feat, hot, nt, preferred_element_type=F32)
        by_row = by_lane.T
        used = lax.broadcasted_iota(jnp.int32, (1, SLOTS), 1) + step * SLOTS < count
        plane = (by_lane[0:1] * N + by_lane[1:2]).astype(jnp.int32)
        plane = jnp.where(used, plane, -1)
        lane = lax.broadcasted_iota(jnp.int32, (SLOTS, LANES), 1)
        hit = lane == by_row[:, 2:3].astype(jnp.int32)
        spread = [jnp.where(hit, by_row[:, n : n + 1], 0.0) for n in range(3, 7)]
        spread = jnp.concatenate(spread, axis=1).astype(BF16)

        def rows_of(block, inner):
            start = pl.multiple_of(block * 256, 256)
            at = lax.broadcasted_iota(jnp.int32, (256, SLOTS), 0) + start
            pick = jnp.where(at == plane, 1.0, 0.0).astype(BF16)
            got = jnp.dot(pick, spread, preferred_element_type=F32)
            for part in range(2):
                one = got[:, 2 * part * LANES : (2 * part + 1) * LANES]
                one = one + got[:, (2 * part + 1) * LANES : (2 * part + 2) * LANES]
                old = out_ref[part, pl.ds(start, 256), :]
                out_ref[part, pl.ds(start, 256), :] = jnp.where(step > 0, old, 0.0) + one
            return inner

        return lax.fori_loop(0, ROWS // 512, rows_of, carry)

    lax.fori_loop(0, jnp.maximum(1, (count + SLOTS - 1) // SLOTS), chunk, 0)


def place(box, cells, weights):
    groups = cells.shape[-1] // 128
    return pl.pallas_call(
        place_kernel,
        out_shape=jax.ShapeDtypeStruct((2, ROWS // 2, LANES), F32),
        in_specs=[pl.BlockSpec(memory_space=pltpu.SMEM)]
        + [pl.BlockSpec(memory_space=pltpu.VMEM)] * 2,
        out_specs=pl.BlockSpec(memory_space=pltpu.VMEM),
        scratch_shapes=[pltpu.VMEM((groups, 128), jnp.int32), pltpu.VMEM((8, groups, 128), F32)],
    )(box, cells.reshape(groups, 128), weights.reshape(2, groups, 128))


def series_kernel(
    remote,
    eig_ref, pair_ref, wave_ref, fwd_ref, inv_ref, zmed_ref, source_ref, medium_hbm, adjoint_hbm,
    out_hbm, grad_ref,
    fre, fim, drive, one, two, kre, kim, pot, medium, adjoint, out,
    xface, yface, zface, zratio, sums, zcor, recv, gsend, grecv,
    send_sem, recv_sem, gsend_sem, grecv_sem, out_sem, in_sem,
):
    load_medium = pltpu.make_async_copy(medium_hbm, medium, in_sem.at[0])
    load_adjoint = pltpu.make_async_copy(adjoint_hbm, adjoint, in_sem.at[1])
    load_medium.start()
    load_adjoint.start()
    if remote:
        space, me = lax.axis_index("space"), lax.axis_index("src")
        bx, by, bz = space // (BGY * BGZ), space // BGZ % BGY, space % BGZ
        below = (
            lax.rem(bx + BGX - 1, BGX) * (BGY * BGZ) + by * BGZ + bz,
            bx * (BGY * BGZ) + lax.rem(by + BGY - 1, BGY) * BGZ + bz,
            bx * (BGY * BGZ) + by * BGZ + lax.rem(bz + BGZ - 1, BGZ),
        )
        above = (
            lax.rem(bx + 1, BGX) * (BGY * BGZ) + by * BGZ + bz,
            bx * (BGY * BGZ) + lax.rem(by + 1, BGY) * BGZ + bz,
            bx * (BGY * BGZ) + by * BGZ + lax.rem(bz + 1, BGZ),
        )
        has_below = [(v > 0).astype(F32) for v in (bx, by, bz)]
        has_above = [(v < e - 1).astype(F32) for v, e in ((bx, BGX), (by, BGY), (bz, BGZ))]
        barrier = pltpu.get_barrier_semaphore()
        for d in range(3):
            for other in (below[d], above[d]):
                pl.semaphore_signal(barrier, 1, device_id={"space": other}, device_id_type=MESH)
        for k in range(1, SRC):
            pl.semaphore_signal(
                barrier, 1, device_id={"src": lax.rem(me + k, SRC)}, device_id_type=MESH
            )
    else:
        me = 0

    low = lower_half(N)

    def table(z, carry):
        rows = pl.ds(pl.multiple_of(z * N, N), N)
        shifted = pair_ref[...] + eig_ref[z]
        scale = 1.0 / ((shifted * shifted + DAMP * DAMP) * float(N**3))
        kre[rows, :] = shifted * scale
        kim[rows, :] = jnp.where(low, -DAMP, DAMP) * scale
        return carry

    lax.fori_loop(0, N, table, 0)

    def half_rows(pair):
        return pl.ds(pl.multiple_of(pair * N, N), N)

    def plane_rows(pair, half):
        return pl.ds(pl.multiple_of((2 * pair + half) * N, N), N)

    def pitched(pair, half):
        return pl.ds(pl.multiple_of((2 * pair + half) * PITCH, 8), N)

    def put_drive(pair, re, im):
        for half, rows in enumerate(trade(re, im)):
            drive[plane_rows(pair, half), :] = rows

    def begin(pair, carry):
        rows = half_rows(pair)
        fre[rows, :] = jnp.zeros((N, LANES), F32)
        fim[rows, :] = jnp.zeros((N, LANES), F32)
        put_drive(pair, source_ref[0, rows, :], source_ref[1, rows, :])
        return carry

    lax.fori_loop(0, N // 2, begin, 0)
    zface[...] = jnp.zeros_like(zface)
    zcor[...] = jnp.zeros_like(zcor)
    for face in range(2):
        zratio[face] = jnp.where(low, -1.0 / DAMP, 1.0 / DAMP) * (zmed_ref[face] - 1.0)

    load_medium.wait()

    def potential(pair, carry):
        both = [medium[plane_rows(pair, half), :] - 1.0 for half in range(2)]
        pot[half_rows(pair), :] = jnp.concatenate(both, axis=1)
        return carry

    lax.fori_loop(0, N // 2, potential, 0)

    if remote:
        pl.semaphore_wait(barrier, 6 + SRC - 1)

    def forward():
        def load(p, _):
            start = p * ITEM
            return along_lanes(drive[pl.ds(start, ITEM), :], fwd_ref[...])

        def store(p, values):
            values = swapped(values)
            for n in range(ITEM // N):
                x = p * (ITEM // N) + n
                extra = (
                    zcor[0, pl.ds(x, 1), :]
                    + wave_ref[0] * zcor[1, pl.ds(x, 1), :]
                    + wave_ref[1] * zcor[2, pl.ds(x, 1), :]
                )
                to = pl.ds(x * PITCH, N)
                one[to, :] = values[n * N : (n + 1) * N] + extra

        staggered(ROWS // ITEM, (load, store))

    def middle():
        def strided(p, n):
            return pl.ds(p * (ITEM // N) + n, N, stride=PITCH)

        def load(p, _):
            values = [one[strided(p, n), :] for n in range(ITEM // N)]
            return along_lanes(jnp.concatenate(values, axis=0), fwd_ref[...])

        def swap(p, values):
            return swapped(values)

        def product(p, values):
            values = along_lanes(values, fwd_ref[...])
            rows = pl.ds(p * ITEM, ITEM)
            return kre[rows, :] * pltpu.roll(values, N, 1) - kim[rows, :] * values

        def back(p, values):
            return along_lanes(values, fwd_ref[...])

        def store(p, values):
            values = along_lanes(values, fwd_ref[...])
            for n in range(ITEM // N):
                two[strided(p, n), :] = values[n * N : (n + 1) * N]

        staggered(ROWS // ITEM, (load, swap, product, back, swap, store))

    def back_swap(item, ends):
        planes = []
        for n in range(BACK // N):
            x = item * (BACK // N) + n
            plane = two[pl.ds(pl.multiple_of(x * PITCH, 8), N), :]
            planes.append(plane)
            if ends:
                sums[0, pl.ds(x, 1), :] = jnp.sum(plane, axis=0, keepdims=True)
                for part in range(2):
                    waved = jnp.sum(wave_ref[part] * plane, axis=0, keepdims=True)
                    sums[1 + part, pl.ds(x, 1), :] = waved
        return swapped(jnp.concatenate(planes, axis=0), exchange=True)

    def updated(pair, even, odd):
        rows = half_rows(pair)
        gre, gim = trade(even, odd)
        ratio = pot[rows, :] * (1.0 / DAMP)
        return gre + ratio * (fim[rows, :] - gim), gim - ratio * (fre[rows, :] - gre)

    def finish_term(step):
        def z_pass(i, inner):
            def load(p, _):
                return back_swap(i * BACKS + p, True)

            def update(p, values):
                values = along_lanes(values, inv_ref[...])
                for n in range(BACK // LANES):
                    pair = (i * BACKS + p) * (BACK // LANES) + n
                    rows = half_rows(pair)
                    re, im = updated(pair, *(values[(2 * n + h) * N : (2 * n + h + 1) * N] for h in range(2)))
                    fre[rows, :] = re
                    fim[rows, :] = im
                    put_drive(
                        pair,
                        pot[rows, :] * re + DAMP * im + source_ref[0, rows, :],
                        pot[rows, :] * im - DAMP * re + source_ref[1, rows, :],
                    )

            staggered(BACKS, (load, update))
            return inner

        lax.fori_loop(0, ROWS // BACK // BACKS, z_pass, 0)

        turned = lambda values: pltpu.roll(values, N, 1)
        greens = (
            turned(sums[0]),
            turned(sums[1]) + jnp.where(low, sums[2], -sums[2]),
        )
        for face in range(2):
            zface[face] = greens[face] - zratio[face] * turned(zface[face] - greens[face])
        first, last = pl.ds(0, N), pl.ds(ROWS // 2 - N, N)
        xface[0] = jnp.where(low, fre[first, :], turned(fim[first, :]))
        xface[1] = jnp.where(low, turned(fre[last, :]), fim[last, :])
        half = N // 2
        for face, row in ((0, 0), (1, N - 1)):
            yface[face, :half] = fre[pl.ds(row, half, stride=N), :]
            yface[face, half:] = fim[pl.ds(row, half, stride=N), :]
        faces = (xface, yface, zface)
        copies = {}
        if remote:
            for d in (1, 2, 0):
                for side, other in ((1, above[d]), (0, below[d])):
                    slot = 1 - side
                    copies[d, slot] = pltpu.make_async_remote_copy(
                        src_ref=faces[d].at[side],
                        dst_ref=recv.at[step, 2 * d + slot],
                        send_sem=send_sem.at[step, 2 * d + slot],
                        recv_sem=recv_sem.at[step, 2 * d + slot],
                        device_id={"space": other},
                        device_id_type=MESH,
                    )
                    copies[d, slot].start()

        def difference(d, slot):
            if not remote:
                return -faces[d][1 - slot]
            copies[d, slot].wait_recv()
            there = (has_below if slot == 0 else has_above)[d]
            return there * recv[step, 2 * d + slot] - faces[d][1 - slot]

        zcor[0] = difference(2, 0)
        upper_end = difference(2, 1)
        zcor[1] = upper_end
        zcor[2] = jnp.where(low, -1.0, 1.0) * turned(upper_end)
        for slot, plane in ((0, pl.ds(0, N)), (1, pl.ds(ROWS - N, N))):
            drive[plane, :] = drive[plane, :] + difference(0, slot)
        for slot, row in ((0, 0), (1, N - 1)):
            gain = difference(1, slot)
            for x2, rows in enumerate(trade(gain[:half], gain[half:])):
                at = pl.ds(x2 * N + row, half, stride=LANES)
                drive[at, :] = drive[at, :] + rows
        for copy in copies.values():
            copy.wait_send()


    def grad_copy(owner, slot):
        return pltpu.make_async_remote_copy(
            src_ref=gsend.at[owner],
            dst_ref=grecv.at[slot],
            send_sem=gsend_sem.at[owner],
            recv_sem=grecv_sem.at[slot],
            device_id={"src": owner},
            device_id_type=MESH,
        )

    def out_copy(i, part):
        rows = pl.ds(pl.multiple_of(i * CH, CH), CH)
        return pltpu.make_async_copy(
            out.at[part, rows], out_hbm.at[part, rows], out_sem.at[i, part]
        )

    def last_pass(k, carry):
        i = lax.rem(me + 1 + k, SRC)
        items = CH // BACK

        def load(p, _):
            return back_swap(i * items + p, False)

        def update(p, values):
            values = along_lanes(values, inv_ref[...])
            for n in range(BACK // LANES):
                pair = (i * items + p) * (BACK // LANES) + n
                new = updated(pair, *(values[(2 * n + h) * N : (2 * n + h + 1) * N] for h in range(2)))
                terms = []
                for part in range(2):
                    sides = []
                    for half in range(2):
                        rows = plane_rows(pair, half)
                        sides.append(adjoint[part, rows, :].astype(F32))
                        out[part, rows, :] = new[part][:, half * N : (half + 1) * N]
                    terms.append(jnp.concatenate(sides, axis=1) * new[part])
                to = (p * (BACK // LANES) + n) * N
                gsend[i, to : to + N, :] = terms[0] - terms[1]

        staggered(items, (load, update))
        for part in range(2):
            out_copy(i, part).start()
        if remote:

            @pl.when(k < SRC - 1)
            def _():
                grad_copy(i, me).start()

        return carry

    def finish():
        load_adjoint.wait()
        lax.fori_loop(0, SRC, last_pass, 0)
        total = gsend[me]
        if remote:
            for k in range(1, SRC):
                other = lax.rem(me + k, SRC)
                grad_copy(other, other).wait_recv()
                total = total + grecv[other]
        for n in range(SLAB // 2):
            for half in range(2):
                to = (2 * n + half) * N
                grad_ref[to : to + N, :] = total[n * N : (n + 1) * N, half * N : (half + 1) * N]
        if remote:
            for k in range(1, SRC):
                grad_copy(lax.rem(me + k, SRC), me).wait_send()
        for i in range(SRC):
            for part in range(2):
                out_copy(i, part).wait()

    def term(step, carry):
        forward()
        middle()
        pl.when(step < TERMS)(lambda: finish_term(step))
        pl.when(step == TERMS)(finish)
        return carry

    lax.fori_loop(0, TERMS + 1, term, 0)


def series(medium, source, adjoint, remote=True):
    k = np.arange(N)
    eig = 2.0 - 2.0 * np.cos(2.0 * np.pi / N * k)
    pair = (eig[:, None] + np.tile(eig, 2)[None, :] - 1.0).astype(np.float32)
    wave = np.stack([np.cos(2.0 * np.pi / N * k), np.sin(2.0 * np.pi / N * k)])
    wave = np.repeat(wave[:, :, None], LANES, axis=2).astype(np.float32)
    ends = jnp.stack([medium[0, :, :, 0], medium[0, :, :, N - 1]])
    ends = jnp.concatenate([ends, ends], axis=2)
    half = lambda: pltpu.VMEM((ROWS // 2, LANES), F32)
    big = lambda: pltpu.VMEM((ROWS, LANES), F32)
    pitch = lambda: pltpu.VMEM((N * PITCH, LANES), F32)
    planes = lambda *count: pltpu.VMEM(count + (N, LANES), F32)
    vmem, anywhere = pl.BlockSpec(memory_space=pltpu.VMEM), pl.BlockSpec(memory_space=pl.ANY)
    return pl.pallas_call(
        functools.partial(series_kernel, remote),
        out_shape=(
            jax.ShapeDtypeStruct((2, ROWS, N), F32),
            jax.ShapeDtypeStruct((CH, N), F32),
        ),
        in_specs=[pl.BlockSpec(memory_space=pltpu.SMEM)] + [vmem] * 6 + [anywhere] * 2,
        out_specs=(anywhere, vmem),
        scratch_shapes=[
            half(), half(), big(), pitch(), pitch(), big(), big(), half(),
            pltpu.VMEM((ROWS, N), F32),
            pltpu.VMEM((2, ROWS, N), BF16),
            pltpu.VMEM((2, ROWS, N), F32),
            planes(2), planes(2), planes(2), planes(2), planes(3), planes(3), planes(TERMS, 6),
            pltpu.VMEM((SRC, CH // 2, LANES), F32),
            pltpu.VMEM((SRC, CH // 2, LANES), F32),
            pltpu.SemaphoreType.DMA((TERMS, 6)),
            pltpu.SemaphoreType.DMA((TERMS, 6)),
            pltpu.SemaphoreType.DMA((SRC,)),
            pltpu.SemaphoreType.DMA((SRC,)),
            pltpu.SemaphoreType.DMA((SRC, 2)),
            pltpu.SemaphoreType.DMA((2,)),
        ],
        compiler_params=pltpu.CompilerParams(
            collective_id=0 if remote else None,
            has_side_effects=remote,
            vmem_limit_bytes=60 * 1024 * 1024,
        ),
    )(
        jnp.asarray(eig.astype(np.float32)),
        jnp.asarray(pair),
        jnp.asarray(wave),
        jnp.asarray(dft_table(-1.0)),
        jnp.asarray(dft_table(1.0)),
        ends,
        source,
        medium.reshape(ROWS, N),
        adjoint.reshape(2, ROWS, N),
    )


def local(medium, source_cells, source_weights, adjoint):
    box = lax.axis_index("space").astype(jnp.int32).reshape(1)
    source = place(box, source_cells, source_weights)
    field, owned = series(medium, source, adjoint)
    return field.reshape(2, 1, 1, N, N, N), owned.reshape(1, SLAB, N, N)


def solution(mesh):
    placed = (
        P("space", None, None, None),
        P("src", None),
        P(None, "src", None),
        P(None, "src", "space", None, None, None),
    )
    return jax.shard_map(
        local,
        mesh=mesh,
        in_specs=placed,
        out_specs=(P(None, "src", "space", None, None, None), P("space", "src", None, None)),
        check_vma=False,
    )
```

```python
import functools

import jax
import jax.numpy as jnp
import numpy as np
from jax import lax
from jax.experimental import pallas as pl
from jax.experimental.pallas import tpu as pltpu
from jax.sharding import PartitionSpec as P

N = 64
ROWS = N * N
LANES = 2 * N
TERMS = 2
BGX, BGY, BGZ = 2, 4, 4
SRC = 8
SLAB = N // SRC
CH = SLAB * N
DAMP = 0.25
PITCH = 72
BACK, BACKS = 512, 4
ITEM = 2048
MESH = pl.DeviceIdType.MESH
SLOTS = 256
F32, BF16 = jnp.float32, jnp.bfloat16


def split(values):
    high = values.astype(BF16)
    low = (values - high.astype(F32)).astype(BF16)
    return high, low


def dft_table(sign):
    k = np.arange(N)
    phase = 2.0 * np.pi / N * (k[:, None] * k[None, :] % N)
    c, s = np.cos(phase), sign * np.sin(phase)
    w = np.block([[c, s], [-s, c]]).astype(np.float32)
    high = w.astype(BF16)
    low = (w - high.astype(np.float32)).astype(BF16)
    half = np.concatenate([high, low], axis=1)
    return np.concatenate([half, half], axis=0)


def along_lanes(values, table):
    high, low = split(values)
    out = jnp.dot(jnp.concatenate([high, low], axis=1), table, preferred_element_type=F32)
    return out[:, :LANES] + out[:, LANES:]


def lower_half(rows):
    return lax.broadcasted_iota(jnp.int32, (rows, LANES), 1) < N


def trade(first, second):
    lower = lower_half(first.shape[0])
    crossed = pltpu.roll(jnp.where(lower, second, first), N, 1)
    return jnp.where(lower, first, crossed), jnp.where(lower, crossed, second)


def swapped(values, exchange=False):
    blocks = []
    for start in range(0, values.shape[0], LANES):
        turned = values[start : start + LANES].T
        first, second = turned[:N], turned[N:]
        blocks += trade(second, first) if exchange else trade(first, second)
    return jnp.concatenate(blocks, axis=0)


def staggered(count, stages):
    held = {}
    for turn in range(count + len(stages) - 1):
        for n in reversed(range(len(stages))):
            item = turn - n
            if 0 <= item < count:
                held[item] = stages[n](item, held.get(item))


def place_kernel(box_ref, cells_ref, weights_ref, out_ref, pos_ref, feat_ref):
    cells = cells_ref[...] - box_ref[0] * (N * N * N)
    inside = (cells >= 0) & (cells < N * N * N)
    mask = jnp.where(inside, 1.0, 0.0).astype(BF16)
    groups = cells.shape[0]
    i0 = lax.broadcasted_iota(jnp.int32, (128, 128), 0)
    i1 = lax.broadcasted_iota(jnp.int32, (128, 128), 1)
    upper = jnp.where(i0 < i1, 1.0, 0.0).astype(BF16)
    within = jnp.dot(mask, upper, preferred_element_type=F32)
    totals = jnp.dot(mask, jnp.ones((128, 128), BF16), preferred_element_type=F32)
    j0 = lax.broadcasted_iota(jnp.int32, (groups, groups), 0)
    j1 = lax.broadcasted_iota(jnp.int32, (groups, groups), 1)
    before = jnp.where(j1 < j0, 1.0, 0.0).astype(BF16)
    offset = jnp.dot(before, totals.astype(BF16), preferred_element_type=F32)
    pos_ref[...] = jnp.where(inside, (within + offset).astype(jnp.int32), -1)
    count = jnp.sum(jnp.where(inside, 1, 0))
    safe = jnp.where(inside, cells, 0)
    rh, rl = split(weights_ref[0])
    ih, il = split(weights_ref[1])
    rows = (
        (safe >> 13).astype(F32),
        ((safe >> 6) & (N - 1)).astype(F32),
        (((safe >> 12) & 1) * N + (safe & (N - 1))).astype(F32),
        rh.astype(F32),
        rl.astype(F32),
        ih.astype(F32),
        il.astype(F32),
    )
    for n, row in enumerate(rows):
        feat_ref[n] = row

    def chunk(step, carry):
        slot = lax.broadcasted_iota(jnp.int32, (SLOTS, 128), 0) + step * SLOTS
        sub = lax.broadcasted_iota(jnp.int32, (16, 128), 0)
        hots, feats = [], []
        for g in range(groups):
            hots.append(jnp.where(pos_ref[g : g + 1, :] == slot, 1.0, 0.0).astype(BF16))
            f = jnp.zeros((16, 128), F32)
            for n in range(len(rows)):
                f = jnp.where(sub == n, feat_ref[n, g : g + 1, :], f)
            feats.append(f.astype(BF16))
        hot = jnp.concatenate(hots, axis=1)
        feat = jnp.concatenate(feats, axis=1)
        nt = (((1,), (1,)), ((), ()))
        by_lane = lax.dot_general(feat, hot, nt, preferred_element_type=F32)
        by_row = by_lane.T
        used = lax.broadcasted_iota(jnp.int32, (1, SLOTS), 1) + step * SLOTS < count
        plane = (by_lane[0:1] * N + by_lane[1:2]).astype(jnp.int32)
        plane = jnp.where(used, plane, -1)
        lane = lax.broadcasted_iota(jnp.int32, (SLOTS, LANES), 1)
        hit = lane == by_row[:, 2:3].astype(jnp.int32)
        spread = [jnp.where(hit, by_row[:, n : n + 1], 0.0) for n in range(3, 7)]
        spread = jnp.concatenate(spread, axis=1).astype(BF16)

        def rows_of(block, inner):
            start = pl.multiple_of(block * 256, 256)
            at = lax.broadcasted_iota(jnp.int32, (256, SLOTS), 0) + start
            pick = jnp.where(at == plane, 1.0, 0.0).astype(BF16)
            got = jnp.dot(pick, spread, preferred_element_type=F32)
            for part in range(2):
                one = got[:, 2 * part * LANES : (2 * part + 1) * LANES]
                one = one + got[:, (2 * part + 1) * LANES : (2 * part + 2) * LANES]
                old = out_ref[part, pl.ds(start, 256), :]
                out_ref[part, pl.ds(start, 256), :] = jnp.where(step > 0, old, 0.0) + one
            return inner

        return lax.fori_loop(0, ROWS // 512, rows_of, carry)

    lax.fori_loop(0, jnp.maximum(1, (count + SLOTS - 1) // SLOTS), chunk, 0)


def place(box, cells, weights):
    groups = cells.shape[-1] // 128
    return pl.pallas_call(
        place_kernel,
        out_shape=jax.ShapeDtypeStruct((2, ROWS // 2, LANES), F32),
        in_specs=[pl.BlockSpec(memory_space=pltpu.SMEM)]
        + [pl.BlockSpec(memory_space=pltpu.VMEM)] * 2,
        out_specs=pl.BlockSpec(memory_space=pltpu.VMEM),
        scratch_shapes=[pltpu.VMEM((groups, 128), jnp.int32), pltpu.VMEM((8, groups, 128), F32)],
        compiler_params=pltpu.CompilerParams(vmem_limit_bytes=12 * 1024 * 1024),
    )(box, cells.reshape(groups, 128), weights.reshape(2, groups, 128))


def series_kernel(
    remote,
    eig_ref, source_ref, medium_hbm, pair_hbm, wave_hbm, fwd_hbm, inv_hbm, adjoint_hbm,
    out_hbm, grad_ref,
    packed, drive, one, two, kre, kim, pot, medium, pair_ref, wave_ref, fwd_ref, inv_ref, adjoint,
    faces, ratios, ends, turns, sums, zcor, recv, gsend, grecv,
    send_sem, recv_sem, gsend_sem, grecv_sem, out_sem, in_sem,
):
    fre, fim = packed.at[0], packed.at[1]
    loads = [
        pltpu.make_async_copy(there, here, in_sem.at[n])
        for n, (there, here) in enumerate(
            (
                (pair_hbm, pair_ref),
                (medium_hbm, medium),
                (wave_hbm, wave_ref),
                (fwd_hbm, fwd_ref),
                (inv_hbm, inv_ref),
                (adjoint_hbm, adjoint),
            )
        )
    ]
    for load in loads:
        load.start()
    if remote:
        space, me = lax.axis_index("space"), lax.axis_index("src")
        bx, by, bz = space // (BGY * BGZ), space // BGZ % BGY, space % BGZ
        below = (
            lax.rem(bx + BGX - 1, BGX) * (BGY * BGZ) + by * BGZ + bz,
            bx * (BGY * BGZ) + lax.rem(by + BGY - 1, BGY) * BGZ + bz,
            bx * (BGY * BGZ) + by * BGZ + lax.rem(bz + BGZ - 1, BGZ),
        )
        above = (
            lax.rem(bx + 1, BGX) * (BGY * BGZ) + by * BGZ + bz,
            bx * (BGY * BGZ) + lax.rem(by + 1, BGY) * BGZ + bz,
            bx * (BGY * BGZ) + by * BGZ + lax.rem(bz + 1, BGZ),
        )
        has_below = [(v > 0).astype(F32) for v in (bx, by, bz)]
        has_above = [(v < e - 1).astype(F32) for v, e in ((bx, BGX), (by, BGY), (bz, BGZ))]
        barrier = pltpu.get_barrier_semaphore()
        for d in range(3):
            for other in (below[d], above[d]):
                pl.semaphore_signal(barrier, 1, device_id={"space": other}, device_id_type=MESH)
        for k in range(1, SRC):
            pl.semaphore_signal(
                barrier, 1, device_id={"src": lax.rem(me + k, SRC)}, device_id_type=MESH
            )
    else:
        me = 0

    low = lower_half(N)

    def table(z, carry):
        rows = pl.ds(pl.multiple_of(z * N, N), N)
        shifted = pair_ref[...] + eig_ref[z]
        scale = 1.0 / ((shifted * shifted + DAMP * DAMP) * float(N**3))
        kre[rows, :] = shifted * scale
        kim[rows, :] = jnp.where(low, -DAMP, DAMP) * scale
        return carry

    loads[0].wait()
    lax.fori_loop(0, N, table, 0)

    def half_rows(pair):
        return pl.ds(pl.multiple_of(pair * N, N), N)

    def plane_rows(pair, half):
        return pl.ds(pl.multiple_of((2 * pair + half) * N, N), N)

    def pitched(pair, half):
        return pl.ds(pl.multiple_of((2 * pair + half) * PITCH, 8), N)

    def put_drive(pair, re, im):
        for half, rows in enumerate(trade(re, im)):
            drive[plane_rows(pair, half), :] = rows

    def begin(pair, carry):
        rows = half_rows(pair)
        fre[rows, :] = jnp.zeros((N, LANES), F32)
        fim[rows, :] = jnp.zeros((N, LANES), F32)
        put_drive(pair, source_ref[0, rows, :], source_ref[1, rows, :])
        return carry

    lax.fori_loop(0, N // 2, begin, 0)
    faces[...] = jnp.zeros_like(faces)
    zcor[...] = jnp.zeros_like(zcor)
    lane = lax.broadcasted_iota(jnp.int32, (N, LANES), 1)

    loads[1].wait()

    def potential(pair, carry):
        both = [medium[plane_rows(pair, half), :] - 1.0 for half in range(2)]
        both = jnp.concatenate(both, axis=1)
        pot[half_rows(pair), :] = both
        moved = pltpu.roll(both, 1 + 2 * pair, 1)
        ends[...] = jnp.where((lane % N) // 2 == pair, moved, ends[...])
        return carry

    lax.fori_loop(0, N // 2, potential, 0)
    turns[...] = jnp.concatenate([ends[...], ends[...]], axis=0).T
    half = N // 2
    for face, (even, odd) in enumerate(((1, N + 1), (N, 0))):
        ratios[2, face, pl.ds(0, half, stride=2), :] = turns[pl.ds(even, half, stride=2), :]
        ratios[2, face, pl.ds(1, half, stride=2), :] = turns[pl.ds(odd, half, stride=2), :]
    for d, planes in (
        (0, (pl.ds(0, N), pl.ds(ROWS - N, N))),
        (1, (pl.ds(0, N, stride=N), pl.ds(N - 1, N, stride=N))),
    ):
        for face in range(2):
            plane = medium[planes[face], :] - 1.0
            ratios[d, face] = jnp.concatenate([plane, plane], axis=1)
    ratios[...] = jnp.where(lower_half(N), -1.0 / DAMP, 1.0 / DAMP) * ratios[...]

    for load in loads[2:5]:
        load.wait()
    if remote:
        pl.semaphore_wait(barrier, 6 + SRC - 1)

    def forward():
        def load(p, _):
            start = p * ITEM
            return along_lanes(drive[pl.ds(start, ITEM), :], fwd_ref[...])

        def store(p, values):
            values = swapped(values)
            for n in range(ITEM // N):
                x = p * (ITEM // N) + n
                extra = (
                    zcor[0, pl.ds(x, 1), :]
                    + wave_ref[0] * zcor[1, pl.ds(x, 1), :]
                    + wave_ref[1] * zcor[2, pl.ds(x, 1), :]
                )
                to = pl.ds(x * PITCH, N)
                one[to, :] = values[n * N : (n + 1) * N] + extra

        staggered(ROWS // ITEM, (load, store))

    def middle():
        def strided(p, n):
            return pl.ds(p * (ITEM // N) + n, N, stride=PITCH)

        def load(p, _):
            values = [one[strided(p, n), :] for n in range(ITEM // N)]
            return along_lanes(jnp.concatenate(values, axis=0), fwd_ref[...])

        def swap(p, values):
            return swapped(values)

        def product(p, values):
            values = along_lanes(values, fwd_ref[...])
            rows = pl.ds(p * ITEM, ITEM)
            return kre[rows, :] * pltpu.roll(values, N, 1) - kim[rows, :] * values

        def back(p, values):
            return along_lanes(values, fwd_ref[...])

        def store(p, values):
            values = along_lanes(values, fwd_ref[...])
            for n in range(ITEM // N):
                two[strided(p, n), :] = values[n * N : (n + 1) * N]

        staggered(ROWS // ITEM, (load, swap, product, back, swap, store))

    def back_swap(item, ends):
        planes = []
        for n in range(BACK // N):
            x = item * (BACK // N) + n
            plane = two[pl.ds(pl.multiple_of(x * PITCH, 8), N), :]
            planes.append(plane)
            if ends:
                sums[0, pl.ds(x, 1), :] = jnp.sum(plane, axis=0, keepdims=True)
                for part in range(2):
                    waved = jnp.sum(wave_ref[part] * plane, axis=0, keepdims=True)
                    sums[1 + part, pl.ds(x, 1), :] = waved
        return swapped(jnp.concatenate(planes, axis=0), exchange=True)

    def back_rows(item):
        return pl.ds(pl.multiple_of(item * BACK, BACK), BACK)

    def updated(pair, even, odd):
        rows = half_rows(pair)
        gre, gim = trade(even, odd)
        ratio = pot[rows, :] * (1.0 / DAMP)
        return gre + ratio * (fim[rows, :] - gim), gim - ratio * (fre[rows, :] - gre)

    def finish_term(step):
        def swap_pass(i, inner):
            for p in range(BACKS):
                one[back_rows(i * BACKS + p), :] = back_swap(i * BACKS + p, True)
            return inner

        lax.fori_loop(0, ROWS // BACK // BACKS, swap_pass, 0)

        turned = lambda values: pltpu.roll(values, N, 1)
        edges = (
            (pl.ds(0, N), pl.ds(ROWS - N, N)),
            (pl.ds(0, N, stride=N), pl.ds(N - 1, N, stride=N)),
        )
        rows = [one[edges[d][face], :] for d in range(2) for face in range(2)]
        rows = along_lanes(jnp.concatenate(rows, axis=0), inv_ref[...])
        greens = (
            (rows[:N], rows[N : 2 * N]),
            (rows[2 * N : 3 * N], rows[3 * N :]),
            (turned(sums[0]), turned(sums[1]) + jnp.where(low, sums[2], -sums[2])),
        )
        copies = {}
        for d in (1, 2, 0):
            for face in range(2):
                green = greens[d][face]
                faces[d, face] = green - ratios[d, face] * turned(faces[d, face] - green)
            if remote:
                for side, other in ((1, above[d]), (0, below[d])):
                    slot = 1 - side
                    copies[d, slot] = pltpu.make_async_remote_copy(
                        src_ref=faces.at[d, side],
                        dst_ref=recv.at[step, 2 * d + slot],
                        send_sem=send_sem.at[step, 2 * d + slot],
                        recv_sem=recv_sem.at[step, 2 * d + slot],
                        device_id={"space": other},
                        device_id_type=MESH,
                    )
                    copies[d, slot].start()

        def z_pass(i, inner):
            def load(p, _):
                return along_lanes(one[back_rows(i * BACKS + p), :], inv_ref[...])

            def update(p, values):
                for n in range(BACK // LANES):
                    pair = (i * BACKS + p) * (BACK // LANES) + n
                    rows = half_rows(pair)
                    re, im = updated(pair, *(values[(2 * n + h) * N : (2 * n + h + 1) * N] for h in range(2)))
                    fre[rows, :] = re
                    fim[rows, :] = im
                    put_drive(
                        pair,
                        pot[rows, :] * re + DAMP * im + source_ref[0, rows, :],
                        pot[rows, :] * im - DAMP * re + source_ref[1, rows, :],
                    )

            staggered(BACKS, (load, update))
            return inner

        lax.fori_loop(0, ROWS // BACK // BACKS, z_pass, 0)

        def difference(d, slot):
            if not remote:
                return -faces[d, 1 - slot]
            copies[d, slot].wait_recv()
            there = (has_below if slot == 0 else has_above)[d]
            return there * recv[step, 2 * d + slot] - faces[d, 1 - slot]

        for d in (0, 1):
            for slot in range(2):
                drive[edges[d][slot], :] = drive[edges[d][slot], :] + difference(d, slot)
        zcor[0] = difference(2, 0)
        upper_end = difference(2, 1)
        zcor[1] = upper_end
        zcor[2] = jnp.where(low, -1.0, 1.0) * turned(upper_end)
        for copy in copies.values():
            copy.wait_send()

    def grad_copy(owner, slot):
        return pltpu.make_async_remote_copy(
            src_ref=gsend.at[owner],
            dst_ref=grecv.at[slot],
            send_sem=gsend_sem.at[owner],
            recv_sem=grecv_sem.at[slot],
            device_id={"src": owner},
            device_id_type=MESH,
        )

    def out_copy(i, part):
        rows = pl.ds(pl.multiple_of(i * (CH // 2), CH // 2), CH // 2)
        return pltpu.make_async_copy(
            packed.at[part, rows], out_hbm.at[part, rows], out_sem.at[i, part]
        )

    def last_pass(k, carry):
        i = lax.rem(me + 1 + k, SRC)
        items = CH // BACK

        def load(p, _):
            return back_swap(i * items + p, False)

        def update(p, values):
            values = along_lanes(values, inv_ref[...])
            for n in range(BACK // LANES):
                pair = (i * items + p) * (BACK // LANES) + n
                new = updated(pair, *(values[(2 * n + h) * N : (2 * n + h + 1) * N] for h in range(2)))
                fre[half_rows(pair), :] = new[0]
                fim[half_rows(pair), :] = new[1]
                terms = []
                for part in range(2):
                    sides = [adjoint[part, plane_rows(pair, half), :].astype(F32) for half in range(2)]
                    terms.append(jnp.concatenate(sides, axis=1) * new[part])
                to = (p * (BACK // LANES) + n) * N
                gsend[i, to : to + N, :] = terms[0] - terms[1]

        staggered(items, (load, update))
        for part in range(2):
            out_copy(i, part).start()
        if remote:

            @pl.when(k < SRC - 1)
            def _():
                grad_copy(i, me).start()

        return carry

    def finish():
        loads[5].wait()
        lax.fori_loop(0, SRC, last_pass, 0)
        total = gsend[me]
        if remote:
            for k in range(1, SRC):
                other = lax.rem(me + k, SRC)
                grad_copy(other, other).wait_recv()
                total = total + grecv[other]
        for n in range(SLAB // 2):
            for half in range(2):
                to = (2 * n + half) * N
                grad_ref[to : to + N, :] = total[n * N : (n + 1) * N, half * N : (half + 1) * N]
        if remote:
            for k in range(1, SRC):
                grad_copy(lax.rem(me + k, SRC), me).wait_send()
        for i in range(SRC):
            for part in range(2):
                out_copy(i, part).wait()

    def term(step, carry):
        forward()
        middle()
        pl.when(step < TERMS)(lambda: finish_term(step))
        pl.when(step == TERMS)(finish)
        return carry

    lax.fori_loop(0, TERMS + 1, term, 0)


def series(medium, source, adjoint, remote=True):
    k = np.arange(N)
    eig = 2.0 - 2.0 * np.cos(2.0 * np.pi / N * k)
    pair = (eig[:, None] + np.tile(eig, 2)[None, :] - 1.0).astype(np.float32)
    wave = np.stack([np.cos(2.0 * np.pi / N * k), np.sin(2.0 * np.pi / N * k)])
    wave = np.repeat(wave[:, :, None], LANES, axis=2).astype(np.float32)
    half = (ROWS // 2, LANES)
    big = lambda: pltpu.VMEM((ROWS, LANES), F32)
    pitch = lambda: pltpu.VMEM((N * PITCH, LANES), F32)
    planes = lambda *count: pltpu.VMEM(count + (N, LANES), F32)
    vmem, anywhere = pl.BlockSpec(memory_space=pltpu.VMEM), pl.BlockSpec(memory_space=pl.ANY)
    hbm = pl.BlockSpec(memory_space=pltpu.HBM)
    return pl.pallas_call(
        functools.partial(series_kernel, remote),
        out_shape=(
            jax.ShapeDtypeStruct((2,) + half, F32),
            jax.ShapeDtypeStruct((CH, N), F32),
        ),
        in_specs=[pl.BlockSpec(memory_space=pltpu.SMEM)] + [vmem] + [hbm] * 6,
        out_specs=(anywhere, vmem),
        scratch_shapes=[
            pltpu.VMEM((2,) + half, F32),
            big(), pitch(), pitch(), big(), big(),
            pltpu.VMEM(half, F32),
            pltpu.VMEM((ROWS, N), F32),
            planes(), planes(2),
            pltpu.VMEM((2 * LANES, 2 * LANES), BF16), pltpu.VMEM((2 * LANES, 2 * LANES), BF16),
            pltpu.VMEM((2, ROWS, N), BF16),
            planes(3, 2), planes(3, 2), planes(), pltpu.VMEM((LANES, LANES), F32),
            planes(3), planes(3), planes(TERMS, 6),
            pltpu.VMEM((SRC, CH // 2, LANES), F32),
            pltpu.VMEM((SRC, CH // 2, LANES), F32),
            pltpu.SemaphoreType.DMA((TERMS, 6)),
            pltpu.SemaphoreType.DMA((TERMS, 6)),
            pltpu.SemaphoreType.DMA((SRC,)),
            pltpu.SemaphoreType.DMA((SRC,)),
            pltpu.SemaphoreType.DMA((SRC, 2)),
            pltpu.SemaphoreType.DMA((6,)),
        ],
        compiler_params=pltpu.CompilerParams(
            collective_id=0 if remote else None,
            has_side_effects=remote,
            vmem_limit_bytes=48 * 1024 * 1024,
        ),
    )(
        jnp.asarray(eig.astype(np.float32)),
        source,
        medium.reshape(ROWS, N),
        jnp.asarray(pair),
        jnp.asarray(wave),
        jnp.asarray(dft_table(-1.0)),
        jnp.asarray(dft_table(1.0)),
        adjoint.reshape(2, ROWS, N),
    )


def unpack_kernel(in_ref, out_ref):
    for part in range(2):
        for n in range(in_ref.shape[1] // N):
            pair = in_ref[part, n * N : (n + 1) * N, :]
            for half in range(2):
                to = (2 * n + half) * N
                out_ref[part, to : to + N, :] = pair[:, half * N : (half + 1) * N]


def unpack(packed, steps=4):
    rows = ROWS // steps
    return pl.pallas_call(
        unpack_kernel,
        grid=(steps,),
        out_shape=jax.ShapeDtypeStruct((2, ROWS, N), F32),
        in_specs=[pl.BlockSpec((2, rows // 2, LANES), lambda i: (0, i, 0))],
        out_specs=pl.BlockSpec((2, rows, N), lambda i: (0, i, 0)),
        compiler_params=pltpu.CompilerParams(vmem_limit_bytes=12 * 1024 * 1024),
    )(packed)


def local(medium, source_cells, source_weights, adjoint):
    box = lax.axis_index("space").astype(jnp.int32).reshape(1)
    source = place(box, source_cells, source_weights)
    packed, owned = series(medium, source, adjoint)
    return unpack(packed).reshape(2, 1, 1, N, N, N), owned.reshape(1, SLAB, N, N)


def solution(mesh):
    placed = (
        P("space", None, None, None),
        P("src", None),
        P(None, "src", None),
        P(None, "src", "space", None, None, None),
    )
    return jax.shard_map(
        local,
        mesh=mesh,
        in_specs=placed,
        out_specs=(P(None, "src", "space", None, None, None), P("space", "src", None, None)),
        check_vma=False,
    )
```

```python
import functools

import jax
import jax.numpy as jnp
import numpy as np
from jax import lax
from jax.experimental import pallas as pl
from jax.experimental.pallas import tpu as pltpu
from jax.sharding import PartitionSpec as P

N = 64
ROWS = N * N
LANES = 2 * N
TERMS = 2
BGX, BGY, BGZ = 2, 4, 4
SRC = 8
SLAB = N // SRC
CH = SLAB * N
DAMP = 0.25
PITCH = 72
BACK, BACKS = 512, 4
ITEM = 2048
MESH = pl.DeviceIdType.MESH
SLOTS = 256
F32, BF16 = jnp.float32, jnp.bfloat16


def split(values):
    high = values.astype(BF16)
    low = (values - high.astype(F32)).astype(BF16)
    return high, low


def dft_table(sign):
    k = np.arange(N)
    phase = 2.0 * np.pi / N * (k[:, None] * k[None, :] % N)
    c, s = np.cos(phase), sign * np.sin(phase)
    w = np.block([[c, s], [-s, c]]).astype(np.float32)
    high = w.astype(BF16)
    low = (w - high.astype(np.float32)).astype(BF16)
    half = np.concatenate([high, low], axis=1)
    return np.concatenate([half, half], axis=0)


def along_lanes(values, table):
    high, low = split(values)
    out = jnp.dot(jnp.concatenate([high, low], axis=1), table, preferred_element_type=F32)
    return out[:, :LANES] + out[:, LANES:]


def lower_half(rows):
    return lax.broadcasted_iota(jnp.int32, (rows, LANES), 1) < N


def trade(first, second):
    lower = lower_half(first.shape[0])
    crossed = pltpu.roll(jnp.where(lower, second, first), N, 1)
    return jnp.where(lower, first, crossed), jnp.where(lower, crossed, second)


def product_swapped(values, table, exchange=False):
    blocks = []
    for start in range(0, values.shape[0], 2 * LANES):
        high, low = split(values[start : start + 2 * LANES])
        both = jnp.concatenate([high, low], axis=1)
        out = lax.dot_general(table, both, (((1,), (1,)), ((), ())), preferred_element_type=F32)
        out = out[:LANES] + out[LANES:]
        for pair in range(out.shape[1] // LANES):
            turned = out[:, pair * LANES : (pair + 1) * LANES]
            first, second = turned[:N], turned[N:]
            blocks += trade(second, first) if exchange else trade(first, second)
    return jnp.concatenate(blocks, axis=0)


def staggered(count, stages):
    held = {}
    for turn in range(count + len(stages) - 1):
        for n in reversed(range(len(stages))):
            item = turn - n
            if 0 <= item < count:
                held[item] = stages[n](item, held.get(item))


def place_kernel(box_ref, cells_ref, weights_ref, out_ref, pos_ref, feat_ref):
    cells = cells_ref[...] - box_ref[0] * (N * N * N)
    inside = (cells >= 0) & (cells < N * N * N)
    mask = jnp.where(inside, 1.0, 0.0).astype(BF16)
    groups = cells.shape[0]
    i0 = lax.broadcasted_iota(jnp.int32, (128, 128), 0)
    i1 = lax.broadcasted_iota(jnp.int32, (128, 128), 1)
    upper = jnp.where(i0 < i1, 1.0, 0.0).astype(BF16)
    within = jnp.dot(mask, upper, preferred_element_type=F32)
    totals = jnp.dot(mask, jnp.ones((128, 128), BF16), preferred_element_type=F32)
    j0 = lax.broadcasted_iota(jnp.int32, (groups, groups), 0)
    j1 = lax.broadcasted_iota(jnp.int32, (groups, groups), 1)
    before = jnp.where(j1 < j0, 1.0, 0.0).astype(BF16)
    offset = jnp.dot(before, totals.astype(BF16), preferred_element_type=F32)
    pos_ref[...] = jnp.where(inside, (within + offset).astype(jnp.int32), -1)
    count = jnp.sum(jnp.where(inside, 1, 0))
    safe = jnp.where(inside, cells, 0)
    rh, rl = split(weights_ref[0])
    ih, il = split(weights_ref[1])
    rows = (
        (safe >> 13).astype(F32),
        ((safe >> 6) & (N - 1)).astype(F32),
        (((safe >> 12) & 1) * N + (safe & (N - 1))).astype(F32),
        rh.astype(F32),
        rl.astype(F32),
        ih.astype(F32),
        il.astype(F32),
    )
    for n, row in enumerate(rows):
        feat_ref[n] = row

    def chunk(step, carry):
        slot = lax.broadcasted_iota(jnp.int32, (SLOTS, 128), 0) + step * SLOTS
        sub = lax.broadcasted_iota(jnp.int32, (16, 128), 0)
        hots, feats = [], []
        for g in range(groups):
            hots.append(jnp.where(pos_ref[g : g + 1, :] == slot, 1.0, 0.0).astype(BF16))
            f = jnp.zeros((16, 128), F32)
            for n in range(len(rows)):
                f = jnp.where(sub == n, feat_ref[n, g : g + 1, :], f)
            feats.append(f.astype(BF16))
        hot = jnp.concatenate(hots, axis=1)
        feat = jnp.concatenate(feats, axis=1)
        nt = (((1,), (1,)), ((), ()))
        by_lane = lax.dot_general(feat, hot, nt, preferred_element_type=F32)
        by_row = by_lane.T
        used = lax.broadcasted_iota(jnp.int32, (1, SLOTS), 1) + step * SLOTS < count
        plane = (by_lane[0:1] * N + by_lane[1:2]).astype(jnp.int32)
        plane = jnp.where(used, plane, -1)
        lane = lax.broadcasted_iota(jnp.int32, (SLOTS, LANES), 1)
        hit = lane == by_row[:, 2:3].astype(jnp.int32)
        spread = [jnp.where(hit, by_row[:, n : n + 1], 0.0) for n in range(3, 7)]
        spread = jnp.concatenate(spread, axis=1).astype(BF16)

        def rows_of(block, inner):
            start = pl.multiple_of(block * 256, 256)
            at = lax.broadcasted_iota(jnp.int32, (256, SLOTS), 0) + start
            pick = jnp.where(at == plane, 1.0, 0.0).astype(BF16)
            got = jnp.dot(pick, spread, preferred_element_type=F32)
            for part in range(2):
                one = got[:, 2 * part * LANES : (2 * part + 1) * LANES]
                one = one + got[:, (2 * part + 1) * LANES : (2 * part + 2) * LANES]
                old = out_ref[part, pl.ds(start, 256), :]
                out_ref[part, pl.ds(start, 256), :] = jnp.where(step > 0, old, 0.0) + one
            return inner

        return lax.fori_loop(0, ROWS // 512, rows_of, carry)

    lax.fori_loop(0, jnp.maximum(1, (count + SLOTS - 1) // SLOTS), chunk, 0)


def place(box, cells, weights):
    groups = cells.shape[-1] // 128
    return pl.pallas_call(
        place_kernel,
        out_shape=jax.ShapeDtypeStruct((2, ROWS // 2, LANES), F32),
        in_specs=[pl.BlockSpec(memory_space=pltpu.SMEM)]
        + [pl.BlockSpec(memory_space=pltpu.VMEM)] * 2,
        out_specs=pl.BlockSpec(memory_space=pltpu.VMEM),
        scratch_shapes=[pltpu.VMEM((groups, 128), jnp.int32), pltpu.VMEM((8, groups, 128), F32)],
        compiler_params=pltpu.CompilerParams(vmem_limit_bytes=12 * 1024 * 1024),
    )(box, cells.reshape(groups, 128), weights.reshape(2, groups, 128))


def series_kernel(
    remote,
    eig_ref, source_ref, medium_hbm, pair_hbm, wave_hbm, fwd_hbm, inv_hbm, turn_hbm, adjoint_hbm,
    out_hbm, grad_ref,
    packed, drive, one, two, kre, kim, pot, medium, pair_ref, wave_ref, fwd_ref, inv_ref, turn_ref, adjoint,
    faces, ratios, ends, turns, sums, zcor, recv, gsend, grecv,
    send_sem, recv_sem, gsend_sem, grecv_sem, out_sem, in_sem,
):
    fre, fim = packed.at[0], packed.at[1]
    loads = [
        pltpu.make_async_copy(there, here, in_sem.at[n])
        for n, (there, here) in enumerate(
            (
                (pair_hbm, pair_ref),
                (medium_hbm, medium),
                (wave_hbm, wave_ref),
                (fwd_hbm, fwd_ref),
                (inv_hbm, inv_ref),
                (turn_hbm, turn_ref),
                (adjoint_hbm, adjoint),
            )
        )
    ]
    for load in loads:
        load.start()
    if remote:
        space, me = lax.axis_index("space"), lax.axis_index("src")
        bx, by, bz = space // (BGY * BGZ), space // BGZ % BGY, space % BGZ
        below = (
            lax.rem(bx + BGX - 1, BGX) * (BGY * BGZ) + by * BGZ + bz,
            bx * (BGY * BGZ) + lax.rem(by + BGY - 1, BGY) * BGZ + bz,
            bx * (BGY * BGZ) + by * BGZ + lax.rem(bz + BGZ - 1, BGZ),
        )
        above = (
            lax.rem(bx + 1, BGX) * (BGY * BGZ) + by * BGZ + bz,
            bx * (BGY * BGZ) + lax.rem(by + 1, BGY) * BGZ + bz,
            bx * (BGY * BGZ) + by * BGZ + lax.rem(bz + 1, BGZ),
        )
        has_below = [(v > 0).astype(F32) for v in (bx, by, bz)]
        has_above = [(v < e - 1).astype(F32) for v, e in ((bx, BGX), (by, BGY), (bz, BGZ))]
        barrier = pltpu.get_barrier_semaphore()
        for d in range(3):
            for other in (below[d], above[d]):
                pl.semaphore_signal(barrier, 1, device_id={"space": other}, device_id_type=MESH)
        for k in range(1, SRC):
            pl.semaphore_signal(
                barrier, 1, device_id={"src": lax.rem(me + k, SRC)}, device_id_type=MESH
            )
    else:
        me = 0

    low = lower_half(N)

    def table(z, carry):
        rows = pl.ds(pl.multiple_of(z * N, N), N)
        shifted = pair_ref[...] + eig_ref[z]
        scale = 1.0 / ((shifted * shifted + DAMP * DAMP) * float(N**3))
        kre[rows, :] = shifted * scale
        kim[rows, :] = jnp.where(low, -DAMP, DAMP) * scale
        return carry

    loads[0].wait()
    lax.fori_loop(0, N, table, 0)

    def half_rows(pair):
        return pl.ds(pl.multiple_of(pair * N, N), N)

    def plane_rows(pair, half):
        return pl.ds(pl.multiple_of((2 * pair + half) * N, N), N)

    def pitched(pair, half):
        return pl.ds(pl.multiple_of((2 * pair + half) * PITCH, 8), N)

    def put_drive(pair, re, im):
        for half, rows in enumerate(trade(re, im)):
            drive[plane_rows(pair, half), :] = rows

    def begin(pair, carry):
        rows = half_rows(pair)
        fre[rows, :] = jnp.zeros((N, LANES), F32)
        fim[rows, :] = jnp.zeros((N, LANES), F32)
        put_drive(pair, source_ref[0, rows, :], source_ref[1, rows, :])
        return carry

    lax.fori_loop(0, N // 2, begin, 0)
    faces[...] = jnp.zeros_like(faces)
    zcor[...] = jnp.zeros_like(zcor)
    lane = lax.broadcasted_iota(jnp.int32, (N, LANES), 1)

    loads[1].wait()

    def potential(pair, carry):
        both = [medium[plane_rows(pair, half), :] - 1.0 for half in range(2)]
        both = jnp.concatenate(both, axis=1)
        pot[half_rows(pair), :] = both
        moved = pltpu.roll(both, 1 + 2 * pair, 1)
        ends[...] = jnp.where((lane % N) // 2 == pair, moved, ends[...])
        return carry

    lax.fori_loop(0, N // 2, potential, 0)
    turns[...] = jnp.concatenate([ends[...], ends[...]], axis=0).T
    half = N // 2
    for face, (even, odd) in enumerate(((1, N + 1), (N, 0))):
        ratios[2, face, pl.ds(0, half, stride=2), :] = turns[pl.ds(even, half, stride=2), :]
        ratios[2, face, pl.ds(1, half, stride=2), :] = turns[pl.ds(odd, half, stride=2), :]
    for d, planes in (
        (0, (pl.ds(0, N), pl.ds(ROWS - N, N))),
        (1, (pl.ds(0, N, stride=N), pl.ds(N - 1, N, stride=N))),
    ):
        for face in range(2):
            plane = medium[planes[face], :] - 1.0
            ratios[d, face] = jnp.concatenate([plane, plane], axis=1)
    ratios[...] = jnp.where(lower_half(N), -1.0 / DAMP, 1.0 / DAMP) * ratios[...]

    for load in loads[2:6]:
        load.wait()

    def forward():
        def load(p, _):
            return product_swapped(drive[pl.ds(p * ITEM, ITEM), :], turn_ref[...])

        def store(p, values):
            for n in range(ITEM // N):
                x = p * (ITEM // N) + n
                extra = (
                    zcor[0, pl.ds(x, 1), :]
                    + wave_ref[0] * zcor[1, pl.ds(x, 1), :]
                    + wave_ref[1] * zcor[2, pl.ds(x, 1), :]
                )
                to = pl.ds(x * PITCH, N)
                one[to, :] = values[n * N : (n + 1) * N] + extra

        staggered(ROWS // ITEM, (load, store))

    def middle():
        def strided(p, n):
            return pl.ds(p * (ITEM // N) + n, N, stride=PITCH)

        def load(p, _):
            values = [one[strided(p, n), :] for n in range(ITEM // N)]
            return product_swapped(jnp.concatenate(values, axis=0), turn_ref[...])

        def product(p, values):
            values = along_lanes(values, fwd_ref[...])
            rows = pl.ds(p * ITEM, ITEM)
            return kre[rows, :] * pltpu.roll(values, N, 1) - kim[rows, :] * values

        def store(p, values):
            values = product_swapped(values, turn_ref[...])
            for n in range(ITEM // N):
                two[strided(p, n), :] = values[n * N : (n + 1) * N]

        staggered(ROWS // ITEM, (load, product, store))

    def back_swap(item, ends):
        planes = []
        for n in range(BACK // N):
            x = item * (BACK // N) + n
            plane = two[pl.ds(pl.multiple_of(x * PITCH, 8), N), :]
            planes.append(plane)
            if ends:
                sums[0, pl.ds(x, 1), :] = jnp.sum(plane, axis=0, keepdims=True)
                for part in range(2):
                    waved = jnp.sum(wave_ref[part] * plane, axis=0, keepdims=True)
                    sums[1 + part, pl.ds(x, 1), :] = waved
        return product_swapped(jnp.concatenate(planes, axis=0), turn_ref[...], exchange=True)

    def back_rows(item):
        return pl.ds(pl.multiple_of(item * BACK, BACK), BACK)

    def updated(pair, even, odd):
        rows = half_rows(pair)
        gre, gim = trade(even, odd)
        ratio = pot[rows, :] * (1.0 / DAMP)
        return gre + ratio * (fim[rows, :] - gim), gim - ratio * (fre[rows, :] - gre)

    def finish_term(step):
        def swap_pass(i, inner):
            for p in range(BACKS):
                one[back_rows(i * BACKS + p), :] = back_swap(i * BACKS + p, True)
            return inner

        lax.fori_loop(0, ROWS // BACK // BACKS, swap_pass, 0)

        turned = lambda values: pltpu.roll(values, N, 1)
        edges = (
            (pl.ds(0, N), pl.ds(ROWS - N, N)),
            (pl.ds(0, N, stride=N), pl.ds(N - 1, N, stride=N)),
        )
        rows = [one[edges[d][face], :] for d in range(2) for face in range(2)]
        rows = along_lanes(jnp.concatenate(rows, axis=0), inv_ref[...])
        total = along_lanes(sums[...].reshape(3 * N, LANES), fwd_ref[...]).reshape(3, N, LANES)
        greens = (
            (rows[:N], rows[N : 2 * N]),
            (rows[2 * N : 3 * N], rows[3 * N :]),
            (turned(total[0]), turned(total[1]) + jnp.where(low, total[2], -total[2])),
        )
        if remote:

            @pl.when(step == 0)
            def _():
                pl.semaphore_wait(barrier, 6 + SRC - 1)

        copies = {}
        for d in (1, 2, 0):
            for face in range(2):
                green = greens[d][face]
                faces[d, face] = green - ratios[d, face] * turned(faces[d, face] - green)
            if remote:
                for side, other in ((1, above[d]), (0, below[d])):
                    slot = 1 - side
                    copies[d, slot] = pltpu.make_async_remote_copy(
                        src_ref=faces.at[d, side],
                        dst_ref=recv.at[step, 2 * d + slot],
                        send_sem=send_sem.at[step, 2 * d + slot],
                        recv_sem=recv_sem.at[step, 2 * d + slot],
                        device_id={"space": other},
                        device_id_type=MESH,
                    )
                    copies[d, slot].start()

        def z_pass(i, inner):
            def load(p, _):
                return along_lanes(one[back_rows(i * BACKS + p), :], inv_ref[...])

            def update(p, values):
                for n in range(BACK // LANES):
                    pair = (i * BACKS + p) * (BACK // LANES) + n
                    rows = half_rows(pair)
                    re, im = updated(pair, *(values[(2 * n + h) * N : (2 * n + h + 1) * N] for h in range(2)))
                    fre[rows, :] = re
                    fim[rows, :] = im
                    put_drive(
                        pair,
                        pot[rows, :] * re + DAMP * im + source_ref[0, rows, :],
                        pot[rows, :] * im - DAMP * re + source_ref[1, rows, :],
                    )

            staggered(BACKS, (load, update))
            return inner

        lax.fori_loop(0, ROWS // BACK // BACKS, z_pass, 0)

        def difference(d, slot):
            if not remote:
                return -faces[d, 1 - slot]
            copies[d, slot].wait_recv()
            there = (has_below if slot == 0 else has_above)[d]
            return there * recv[step, 2 * d + slot] - faces[d, 1 - slot]

        for d in (0, 1):
            for slot in range(2):
                drive[edges[d][slot], :] = drive[edges[d][slot], :] + difference(d, slot)
        zcor[0] = difference(2, 0)
        upper_end = difference(2, 1)
        zcor[1] = upper_end
        zcor[2] = jnp.where(low, -1.0, 1.0) * turned(upper_end)
        for copy in copies.values():
            copy.wait_send()

    def grad_copy(owner, slot):
        return pltpu.make_async_remote_copy(
            src_ref=gsend.at[owner],
            dst_ref=grecv.at[slot],
            send_sem=gsend_sem.at[owner],
            recv_sem=grecv_sem.at[slot],
            device_id={"src": owner},
            device_id_type=MESH,
        )

    def out_copy(i, part):
        rows = pl.ds(pl.multiple_of(i * (CH // 2), CH // 2), CH // 2)
        return pltpu.make_async_copy(
            packed.at[part, rows], out_hbm.at[part, rows], out_sem.at[i, part]
        )

    def last_pass(k, carry):
        i = lax.rem(me // 2 + 2 + lax.rem(k, 4) - k // 4, 4) * 2 + lax.rem(me + 1 - k // 4, 2)
        items = CH // BACK

        def load(p, _):
            return back_swap(i * items + p, False)

        def update(p, values):
            values = along_lanes(values, inv_ref[...])
            for n in range(BACK // LANES):
                pair = (i * items + p) * (BACK // LANES) + n
                new = updated(pair, *(values[(2 * n + h) * N : (2 * n + h + 1) * N] for h in range(2)))
                fre[half_rows(pair), :] = new[0]
                fim[half_rows(pair), :] = new[1]
                terms = []
                for part in range(2):
                    sides = [adjoint[part, plane_rows(pair, half), :].astype(F32) for half in range(2)]
                    terms.append(jnp.concatenate(sides, axis=1) * new[part])
                to = (p * (BACK // LANES) + n) * N
                gsend[i, to : to + N, :] = terms[0] - terms[1]

        staggered(items, (load, update))
        for part in range(2):
            out_copy(i, part).start()
        if remote:

            @pl.when(k < SRC - 1)
            def _():
                grad_copy(i, me).start()

        return carry

    def finish():
        loads[6].wait()
        lax.fori_loop(0, SRC, last_pass, 0)
        total = gsend[me]
        if remote:
            for k in range(1, SRC):
                other = lax.rem(me + k, SRC)
                grad_copy(other, other).wait_recv()
                total = total + grecv[other]
        for n in range(SLAB // 2):
            for half in range(2):
                to = (2 * n + half) * N
                grad_ref[to : to + N, :] = total[n * N : (n + 1) * N, half * N : (half + 1) * N]
        if remote:
            for k in range(1, SRC):
                grad_copy(lax.rem(me + k, SRC), me).wait_send()
        for i in range(SRC):
            for part in range(2):
                out_copy(i, part).wait()

    def term(step, carry):
        forward()
        middle()
        pl.when(step < TERMS)(lambda: finish_term(step))
        pl.when(step == TERMS)(finish)
        return carry

    lax.fori_loop(0, TERMS + 1, term, 0)


def series(medium, source, adjoint, remote=True):
    k = np.arange(N)
    eig = 2.0 - 2.0 * np.cos(2.0 * np.pi / N * k)
    pair = (eig[:, None] + np.tile(eig, 2)[None, :] - 1.0).astype(np.float32)
    wave = np.stack([np.cos(2.0 * np.pi / N * k), np.sin(2.0 * np.pi / N * k)])
    wave = np.repeat(wave[:, :, None], LANES, axis=2).astype(np.float32)
    half = (ROWS // 2, LANES)
    big = lambda: pltpu.VMEM((ROWS, LANES), F32)
    pitch = lambda: pltpu.VMEM((N * PITCH, LANES), F32)
    square = pltpu.VMEM((2 * LANES, 2 * LANES), BF16)
    planes = lambda *count: pltpu.VMEM(count + (N, LANES), F32)
    vmem, anywhere = pl.BlockSpec(memory_space=pltpu.VMEM), pl.BlockSpec(memory_space=pl.ANY)
    hbm = pl.BlockSpec(memory_space=pltpu.HBM)
    return pl.pallas_call(
        functools.partial(series_kernel, remote),
        out_shape=(
            jax.ShapeDtypeStruct((2,) + half, F32),
            jax.ShapeDtypeStruct((CH, N), F32),
        ),
        in_specs=[pl.BlockSpec(memory_space=pltpu.SMEM)] + [vmem] + [hbm] * 7,
        out_specs=(anywhere, vmem),
        scratch_shapes=[
            pltpu.VMEM((2,) + half, F32),
            big(), pitch(), pitch(), big(), big(),
            pltpu.VMEM(half, F32),
            pltpu.VMEM((ROWS, N), F32),
            planes(), planes(2),
            square, square, square,
            pltpu.VMEM((2, ROWS, N), BF16),
            planes(3, 2), planes(3, 2), planes(), pltpu.VMEM((LANES, LANES), F32),
            planes(3), planes(3), planes(TERMS, 6),
            pltpu.VMEM((SRC, CH // 2, LANES), F32),
            pltpu.VMEM((SRC, CH // 2, LANES), F32),
            pltpu.SemaphoreType.DMA((TERMS, 6)),
            pltpu.SemaphoreType.DMA((TERMS, 6)),
            pltpu.SemaphoreType.DMA((SRC,)),
            pltpu.SemaphoreType.DMA((SRC,)),
            pltpu.SemaphoreType.DMA((SRC, 2)),
            pltpu.SemaphoreType.DMA((7,)),
        ],
        compiler_params=pltpu.CompilerParams(
            collective_id=0 if remote else None,
            has_side_effects=remote,
            vmem_limit_bytes=48 * 1024 * 1024,
        ),
    )(
        jnp.asarray(eig.astype(np.float32)),
        source,
        medium.reshape(ROWS, N),
        jnp.asarray(pair),
        jnp.asarray(wave),
        jnp.asarray(dft_table(-1.0)),
        jnp.asarray(dft_table(1.0)),
        jnp.asarray(dft_table(-1.0).T),
        adjoint.reshape(2, ROWS, N),
    )


def unpack_kernel(in_ref, out_ref):
    for part in range(2):
        for n in range(in_ref.shape[1] // N):
            pair = in_ref[part, n * N : (n + 1) * N, :]
            for half in range(2):
                to = (2 * n + half) * N
                out_ref[part, to : to + N, :] = pair[:, half * N : (half + 1) * N]


def unpack(packed, steps=4):
    rows = ROWS // steps
    return pl.pallas_call(
        unpack_kernel,
        grid=(steps,),
        out_shape=jax.ShapeDtypeStruct((2, ROWS, N), F32),
        in_specs=[pl.BlockSpec((2, rows // 2, LANES), lambda i: (0, i, 0))],
        out_specs=pl.BlockSpec((2, rows, N), lambda i: (0, i, 0)),
        compiler_params=pltpu.CompilerParams(vmem_limit_bytes=12 * 1024 * 1024),
    )(packed)


def local(medium, source_cells, source_weights, adjoint):
    box = lax.axis_index("space").astype(jnp.int32).reshape(1)
    source = place(box, source_cells, source_weights)
    packed, owned = series(medium, source, adjoint)
    return unpack(packed).reshape(2, 1, 1, N, N, N), owned.reshape(1, SLAB, N, N)


def solution(mesh):
    placed = (
        P("space", None, None, None),
        P("src", None),
        P(None, "src", None),
        P(None, "src", "space", None, None, None),
    )
    return jax.shard_map(
        local,
        mesh=mesh,
        in_specs=placed,
        out_specs=(P(None, "src", "space", None, None, None), P("space", "src", None, None)),
        check_vma=False,
    )
```

```python
import functools

import jax
import jax.numpy as jnp
import numpy as np
from jax import lax
from jax.experimental import pallas as pl
from jax.experimental.pallas import tpu as pltpu
from jax.sharding import PartitionSpec as P

N = 64
ROWS = N * N
LANES = 2 * N
TERMS = 2
BGX, BGY, BGZ = 2, 4, 4
SRC = 8
SLAB = N // SRC
CH = SLAB * N
DAMP = 0.25
PITCH = 72
BACK, BACKS = 512, 4
ITEM = 2048
MESH = pl.DeviceIdType.MESH
SLOTS = 256
F32, BF16 = jnp.float32, jnp.bfloat16


def split(values):
    high = values.astype(BF16)
    low = (values - high.astype(F32)).astype(BF16)
    return high, low


def dft_table(sign):
    k = np.arange(N)
    phase = 2.0 * np.pi / N * (k[:, None] * k[None, :] % N)
    c, s = np.cos(phase), sign * np.sin(phase)
    w = np.block([[c, s], [-s, c]]).astype(np.float32)
    high = w.astype(BF16)
    low = (w - high.astype(np.float32)).astype(BF16)
    half = np.concatenate([high, low], axis=1)
    return np.concatenate([half, half], axis=0)


def along_lanes(values, table):
    high, low = split(values)
    out = jnp.dot(jnp.concatenate([high, low], axis=1), table, preferred_element_type=F32)
    return out[:, :LANES] + out[:, LANES:]


def lower_half(rows):
    return lax.broadcasted_iota(jnp.int32, (rows, LANES), 1) < N


def trade(first, second):
    lower = lower_half(first.shape[0])
    crossed = pltpu.roll(jnp.where(lower, second, first), N, 1)
    return jnp.where(lower, first, crossed), jnp.where(lower, crossed, second)


def product_swapped(values, table, exchange=False):
    blocks = []
    for start in range(0, values.shape[0], 2 * LANES):
        high, low = split(values[start : start + 2 * LANES])
        both = jnp.concatenate([high, low], axis=1)
        out = lax.dot_general(table, both, (((1,), (1,)), ((), ())), preferred_element_type=F32)
        out = out[:LANES] + out[LANES:]
        for pair in range(out.shape[1] // LANES):
            turned = out[:, pair * LANES : (pair + 1) * LANES]
            first, second = turned[:N], turned[N:]
            blocks += trade(second, first) if exchange else trade(first, second)
    return jnp.concatenate(blocks, axis=0)


def staggered(count, stages):
    held = {}
    for turn in range(count + len(stages) - 1):
        for n in reversed(range(len(stages))):
            item = turn - n
            if 0 <= item < count:
                held[item] = stages[n](item, held.get(item))


def place_kernel(box_ref, cells_ref, weights_ref, out_ref, pos_ref, feat_ref):
    cells = cells_ref[...] - box_ref[0] * (N * N * N)
    inside = (cells >= 0) & (cells < N * N * N)
    mask = jnp.where(inside, 1.0, 0.0).astype(BF16)
    groups = cells.shape[0]
    i0 = lax.broadcasted_iota(jnp.int32, (128, 128), 0)
    i1 = lax.broadcasted_iota(jnp.int32, (128, 128), 1)
    upper = jnp.where(i0 < i1, 1.0, 0.0).astype(BF16)
    within = jnp.dot(mask, upper, preferred_element_type=F32)
    totals = jnp.dot(mask, jnp.ones((128, 128), BF16), preferred_element_type=F32)
    j0 = lax.broadcasted_iota(jnp.int32, (groups, groups), 0)
    j1 = lax.broadcasted_iota(jnp.int32, (groups, groups), 1)
    before = jnp.where(j1 < j0, 1.0, 0.0).astype(BF16)
    offset = jnp.dot(before, totals.astype(BF16), preferred_element_type=F32)
    pos_ref[...] = jnp.where(inside, (within + offset).astype(jnp.int32), -1)
    count = jnp.sum(jnp.where(inside, 1, 0))
    safe = jnp.where(inside, cells, 0)
    rh, rl = split(weights_ref[0])
    ih, il = split(weights_ref[1])
    rows = (
        (safe >> 13).astype(F32),
        ((safe >> 6) & (N - 1)).astype(F32),
        (((safe >> 12) & 1) * N + (safe & (N - 1))).astype(F32),
        rh.astype(F32),
        rl.astype(F32),
        ih.astype(F32),
        il.astype(F32),
    )
    for n, row in enumerate(rows):
        feat_ref[n] = row

    def chunk(step, carry):
        slot = lax.broadcasted_iota(jnp.int32, (SLOTS, 128), 0) + step * SLOTS
        sub = lax.broadcasted_iota(jnp.int32, (16, 128), 0)
        hots, feats = [], []
        for g in range(groups):
            hots.append(jnp.where(pos_ref[g : g + 1, :] == slot, 1.0, 0.0).astype(BF16))
            f = jnp.zeros((16, 128), F32)
            for n in range(len(rows)):
                f = jnp.where(sub == n, feat_ref[n, g : g + 1, :], f)
            feats.append(f.astype(BF16))
        hot = jnp.concatenate(hots, axis=1)
        feat = jnp.concatenate(feats, axis=1)
        nt = (((1,), (1,)), ((), ()))
        by_lane = lax.dot_general(feat, hot, nt, preferred_element_type=F32)
        by_row = by_lane.T
        used = lax.broadcasted_iota(jnp.int32, (1, SLOTS), 1) + step * SLOTS < count
        plane = (by_lane[0:1] * N + by_lane[1:2]).astype(jnp.int32)
        plane = jnp.where(used, plane, -1)
        lane = lax.broadcasted_iota(jnp.int32, (SLOTS, LANES), 1)
        hit = lane == by_row[:, 2:3].astype(jnp.int32)
        spread = [jnp.where(hit, by_row[:, n : n + 1], 0.0) for n in range(3, 7)]
        spread = jnp.concatenate(spread, axis=1).astype(BF16)

        def rows_of(block, inner):
            start = pl.multiple_of(block * 256, 256)
            at = lax.broadcasted_iota(jnp.int32, (256, SLOTS), 0) + start
            pick = jnp.where(at == plane, 1.0, 0.0).astype(BF16)
            got = jnp.dot(pick, spread, preferred_element_type=F32)
            for part in range(2):
                one = got[:, 2 * part * LANES : (2 * part + 1) * LANES]
                one = one + got[:, (2 * part + 1) * LANES : (2 * part + 2) * LANES]
                old = out_ref[part, pl.ds(start, 256), :]
                out_ref[part, pl.ds(start, 256), :] = jnp.where(step > 0, old, 0.0) + one
            return inner

        return lax.fori_loop(0, ROWS // 512, rows_of, carry)

    lax.fori_loop(0, jnp.maximum(1, (count + SLOTS - 1) // SLOTS), chunk, 0)


def place(box, cells, weights):
    groups = cells.shape[-1] // 128
    return pl.pallas_call(
        place_kernel,
        out_shape=jax.ShapeDtypeStruct((2, ROWS // 2, LANES), F32),
        in_specs=[pl.BlockSpec(memory_space=pltpu.SMEM)]
        + [pl.BlockSpec(memory_space=pltpu.VMEM)] * 2,
        out_specs=pl.BlockSpec(memory_space=pltpu.VMEM),
        scratch_shapes=[pltpu.VMEM((groups, 128), jnp.int32), pltpu.VMEM((8, groups, 128), F32)],
        compiler_params=pltpu.CompilerParams(vmem_limit_bytes=12 * 1024 * 1024),
    )(box, cells.reshape(groups, 128), weights.reshape(2, groups, 128))


def series_kernel(
    remote,
    eig_ref, source_ref, medium_hbm, pair_hbm, wave_hbm, fwd_hbm, inv_hbm, turn_hbm, adjoint_hbm,
    out_hbm, grad_ref,
    packed, drive, one, two, kre, kim, pot, medium, pair_ref, wave_ref, fwd_ref, inv_ref, turn_ref, adjoint,
    faces, ratios, ends, turns, sums, zcor, recv, gsend, grecv,
    send_sem, recv_sem, gsend_sem, grecv_sem, out_sem, in_sem,
):
    fre, fim = packed.at[0], packed.at[1]
    loads = [
        pltpu.make_async_copy(there, here, in_sem.at[n])
        for n, (there, here) in enumerate(
            (
                (pair_hbm, pair_ref),
                (medium_hbm, medium),
                (wave_hbm, wave_ref),
                (fwd_hbm, fwd_ref),
                (inv_hbm, inv_ref),
                (turn_hbm, turn_ref),
                (adjoint_hbm, adjoint),
            )
        )
    ]
    for load in loads:
        load.start()
    if remote:
        space, me = lax.axis_index("space"), lax.axis_index("src")
        bx, by, bz = space // (BGY * BGZ), space // BGZ % BGY, space % BGZ
        below = (
            lax.rem(bx + BGX - 1, BGX) * (BGY * BGZ) + by * BGZ + bz,
            bx * (BGY * BGZ) + lax.rem(by + BGY - 1, BGY) * BGZ + bz,
            bx * (BGY * BGZ) + by * BGZ + lax.rem(bz + BGZ - 1, BGZ),
        )
        above = (
            lax.rem(bx + 1, BGX) * (BGY * BGZ) + by * BGZ + bz,
            bx * (BGY * BGZ) + lax.rem(by + 1, BGY) * BGZ + bz,
            bx * (BGY * BGZ) + by * BGZ + lax.rem(bz + 1, BGZ),
        )
        has_below = [(v > 0).astype(F32) for v in (bx, by, bz)]
        has_above = [(v < e - 1).astype(F32) for v, e in ((bx, BGX), (by, BGY), (bz, BGZ))]
        barrier = pltpu.get_barrier_semaphore()
        for d in range(3):
            for other in (below[d], above[d]):
                pl.semaphore_signal(barrier, 1, device_id={"space": other}, device_id_type=MESH)
        for k in range(1, SRC):
            pl.semaphore_signal(
                barrier, 1, device_id={"src": lax.rem(me + k, SRC)}, device_id_type=MESH
            )
    else:
        me = 0

    low = lower_half(N)

    def table(z, carry):
        shifted = pair_ref[...] + eig_ref[z]
        scale = 1.0 / ((shifted * shifted + DAMP * DAMP) * float(N**3))
        real, imag = shifted * scale, jnp.where(low, -DAMP, DAMP) * scale
        for same in (z, lax.rem(N - z, N)):
            rows = pl.ds(pl.multiple_of(same * N, N), N)
            kre[rows, :] = real
            kim[rows, :] = imag
        return carry

    loads[0].wait()
    lax.fori_loop(0, N // 2 + 1, table, 0)

    def half_rows(pair):
        return pl.ds(pl.multiple_of(pair * N, N), N)

    def plane_rows(pair, half):
        return pl.ds(pl.multiple_of((2 * pair + half) * N, N), N)

    def pitched(pair, half):
        return pl.ds(pl.multiple_of((2 * pair + half) * PITCH, 8), N)

    def put_drive(pair, re, im):
        for half, rows in enumerate(trade(re, im)):
            drive[plane_rows(pair, half), :] = rows

    def begin(pair, carry):
        rows = half_rows(pair)
        fre[rows, :] = jnp.zeros((N, LANES), F32)
        fim[rows, :] = jnp.zeros((N, LANES), F32)
        put_drive(pair, source_ref[0, rows, :], source_ref[1, rows, :])
        return carry

    lax.fori_loop(0, N // 2, begin, 0)
    faces[...] = jnp.zeros_like(faces)
    zcor[...] = jnp.zeros_like(zcor)
    lane = lax.broadcasted_iota(jnp.int32, (N, LANES), 1)

    loads[1].wait()

    def potential(pair, carry):
        both = [medium[plane_rows(pair, half), :] - 1.0 for half in range(2)]
        both = jnp.concatenate(both, axis=1)
        pot[half_rows(pair), :] = both
        moved = pltpu.roll(both, 1 + 2 * pair, 1)
        ends[...] = jnp.where((lane % N) // 2 == pair, moved, ends[...])
        return carry

    lax.fori_loop(0, N // 2, potential, 0)
    turns[...] = jnp.concatenate([ends[...], ends[...]], axis=0).T
    half = N // 2
    for face, (even, odd) in enumerate(((1, N + 1), (N, 0))):
        ratios[2, face, pl.ds(0, half, stride=2), :] = turns[pl.ds(even, half, stride=2), :]
        ratios[2, face, pl.ds(1, half, stride=2), :] = turns[pl.ds(odd, half, stride=2), :]
    for d, planes in (
        (0, (pl.ds(0, N), pl.ds(ROWS - N, N))),
        (1, (pl.ds(0, N, stride=N), pl.ds(N - 1, N, stride=N))),
    ):
        for face in range(2):
            plane = medium[planes[face], :] - 1.0
            ratios[d, face] = jnp.concatenate([plane, plane], axis=1)
    ratios[...] = jnp.where(lower_half(N), -1.0 / DAMP, 1.0 / DAMP) * ratios[...]

    for load in loads[2:6]:
        load.wait()

    def forward():
        def load(p, _):
            return product_swapped(drive[pl.ds(p * ITEM, ITEM), :], turn_ref[...])

        def store(p, values):
            for n in range(ITEM // N):
                x = p * (ITEM // N) + n
                extra = (
                    zcor[0, pl.ds(x, 1), :]
                    + wave_ref[0] * zcor[1, pl.ds(x, 1), :]
                    + wave_ref[1] * zcor[2, pl.ds(x, 1), :]
                )
                to = pl.ds(x * PITCH, N)
                one[to, :] = values[n * N : (n + 1) * N] + extra

        staggered(ROWS // ITEM, (load, store))

    def middle():
        def strided(p, n):
            return pl.ds(p * (ITEM // N) + n, N, stride=PITCH)

        def load(p, _):
            values = [one[strided(p, n), :] for n in range(ITEM // N)]
            return product_swapped(jnp.concatenate(values, axis=0), turn_ref[...])

        def product(p, values):
            values = along_lanes(values, fwd_ref[...])
            rows = pl.ds(p * ITEM, ITEM)
            return kre[rows, :] * pltpu.roll(values, N, 1) - kim[rows, :] * values

        def store(p, values):
            values = product_swapped(values, turn_ref[...])
            for n in range(ITEM // N):
                two[strided(p, n), :] = values[n * N : (n + 1) * N]

        staggered(ROWS // ITEM, (load, product, store))

    def back_swap(item, ends):
        planes = []
        for n in range(BACK // N):
            x = item * (BACK // N) + n
            plane = two[pl.ds(pl.multiple_of(x * PITCH, 8), N), :]
            planes.append(plane)
            if ends:
                sums[0, pl.ds(x, 1), :] = jnp.sum(plane, axis=0, keepdims=True)
                for part in range(2):
                    waved = jnp.sum(wave_ref[part] * plane, axis=0, keepdims=True)
                    sums[1 + part, pl.ds(x, 1), :] = waved
        return product_swapped(jnp.concatenate(planes, axis=0), turn_ref[...], exchange=True)

    def back_rows(item):
        return pl.ds(pl.multiple_of(item * BACK, BACK), BACK)

    def updated(pair, even, odd):
        rows = half_rows(pair)
        gre, gim = trade(even, odd)
        ratio = pot[rows, :] * (1.0 / DAMP)
        return gre + ratio * (fim[rows, :] - gim), gim - ratio * (fre[rows, :] - gre)

    def finish_term(step):
        def swap_pass(i, inner):
            for p in range(BACKS):
                one[back_rows(i * BACKS + p), :] = back_swap(i * BACKS + p, True)
            return inner

        lax.fori_loop(0, ROWS // BACK // BACKS, swap_pass, 0)

        turned = lambda values: pltpu.roll(values, N, 1)
        edges = (
            (pl.ds(0, N), pl.ds(ROWS - N, N)),
            (pl.ds(0, N, stride=N), pl.ds(N - 1, N, stride=N)),
        )
        rows = [one[edges[d][face], :] for d in range(2) for face in range(2)]
        rows = along_lanes(jnp.concatenate(rows, axis=0), inv_ref[...])
        total = along_lanes(sums[...].reshape(3 * N, LANES), fwd_ref[...]).reshape(3, N, LANES)
        greens = (
            (rows[:N], rows[N : 2 * N]),
            (rows[2 * N : 3 * N], rows[3 * N :]),
            (turned(total[0]), turned(total[1]) + jnp.where(low, total[2], -total[2])),
        )
        if remote:

            @pl.when(step == 0)
            def _():
                pl.semaphore_wait(barrier, 6 + SRC - 1)

        copies = {}
        for d in (1, 2, 0):
            for face in range(2):
                green = greens[d][face]
                faces[d, face] = green - ratios[d, face] * turned(faces[d, face] - green)
            if remote:
                for side, other in ((1, above[d]), (0, below[d])):
                    slot = 1 - side
                    copies[d, slot] = pltpu.make_async_remote_copy(
                        src_ref=faces.at[d, side],
                        dst_ref=recv.at[step, 2 * d + slot],
                        send_sem=send_sem.at[step, 2 * d + slot],
                        recv_sem=recv_sem.at[step, 2 * d + slot],
                        device_id={"space": other},
                        device_id_type=MESH,
                    )
                    copies[d, slot].start()

        def z_pass(i, inner):
            def load(p, _):
                return along_lanes(one[back_rows(i * BACKS + p), :], inv_ref[...])

            def update(p, values):
                for n in range(BACK // LANES):
                    pair = (i * BACKS + p) * (BACK // LANES) + n
                    rows = half_rows(pair)
                    re, im = updated(pair, *(values[(2 * n + h) * N : (2 * n + h + 1) * N] for h in range(2)))
                    fre[rows, :] = re
                    fim[rows, :] = im
                    put_drive(
                        pair,
                        pot[rows, :] * re + DAMP * im + source_ref[0, rows, :],
                        pot[rows, :] * im - DAMP * re + source_ref[1, rows, :],
                    )

            staggered(BACKS, (load, update))
            return inner

        lax.fori_loop(0, ROWS // BACK // BACKS, z_pass, 0)

        def difference(d, slot):
            if not remote:
                return -faces[d, 1 - slot]
            copies[d, slot].wait_recv()
            there = (has_below if slot == 0 else has_above)[d]
            return there * recv[step, 2 * d + slot] - faces[d, 1 - slot]

        for d in (0, 1):
            for slot in range(2):
                drive[edges[d][slot], :] = drive[edges[d][slot], :] + difference(d, slot)
        zcor[0] = difference(2, 0)
        upper_end = difference(2, 1)
        zcor[1] = upper_end
        zcor[2] = jnp.where(low, -1.0, 1.0) * turned(upper_end)
        for copy in copies.values():
            copy.wait_send()

    def grad_copy(owner, slot):
        return pltpu.make_async_remote_copy(
            src_ref=gsend.at[owner],
            dst_ref=grecv.at[slot],
            send_sem=gsend_sem.at[owner],
            recv_sem=grecv_sem.at[slot],
            device_id={"src": owner},
            device_id_type=MESH,
        )

    def out_copy(i, part):
        rows = pl.ds(pl.multiple_of(i * (CH // 2), CH // 2), CH // 2)
        return pltpu.make_async_copy(
            packed.at[part, rows], out_hbm.at[part, rows], out_sem.at[i, part]
        )

    def last_pass(k, carry):
        i = lax.rem(me // 2 + 2 + lax.rem(k, 4) - k // 4, 4) * 2 + lax.rem(me + 1 - k // 4, 2)
        items = CH // BACK

        def load(p, _):
            return back_swap(i * items + p, False)

        def update(p, values):
            values = along_lanes(values, inv_ref[...])
            for n in range(BACK // LANES):
                pair = (i * items + p) * (BACK // LANES) + n
                new = updated(pair, *(values[(2 * n + h) * N : (2 * n + h + 1) * N] for h in range(2)))
                fre[half_rows(pair), :] = new[0]
                fim[half_rows(pair), :] = new[1]
                terms = []
                for part in range(2):
                    sides = [adjoint[part, plane_rows(pair, half), :].astype(F32) for half in range(2)]
                    terms.append(jnp.concatenate(sides, axis=1) * new[part])
                to = (p * (BACK // LANES) + n) * N
                gsend[i, to : to + N, :] = terms[0] - terms[1]

        staggered(items, (load, update))
        for part in range(2):
            out_copy(i, part).start()
        if remote:

            @pl.when(k < SRC - 1)
            def _():
                grad_copy(i, me).start()

        return carry

    def finish():
        loads[6].wait()
        lax.fori_loop(0, SRC, last_pass, 0)
        total = gsend[me]
        if remote:
            for k in range(1, SRC):
                other = lax.rem(me + k, SRC)
                grad_copy(other, other).wait_recv()
                total = total + grecv[other]
        grad_ref[...] = total
        if remote:
            for k in range(1, SRC):
                grad_copy(lax.rem(me + k, SRC), me).wait_send()
        for i in range(SRC):
            for part in range(2):
                out_copy(i, part).wait()

    def term(step, carry):
        forward()
        middle()
        pl.when(step < TERMS)(lambda: finish_term(step))
        pl.when(step == TERMS)(finish)
        return carry

    lax.fori_loop(0, TERMS + 1, term, 0)


def series(medium, source, adjoint, remote=True):
    k = np.arange(N)
    eig = 2.0 - 2.0 * np.cos(2.0 * np.pi / N * k)
    pair = (eig[:, None] + np.tile(eig, 2)[None, :] - 1.0).astype(np.float32)
    wave = np.stack([np.cos(2.0 * np.pi / N * k), np.sin(2.0 * np.pi / N * k)])
    wave = np.repeat(wave[:, :, None], LANES, axis=2).astype(np.float32)
    half = (ROWS // 2, LANES)
    big = lambda: pltpu.VMEM((ROWS, LANES), F32)
    pitch = lambda: pltpu.VMEM((N * PITCH, LANES), F32)
    square = pltpu.VMEM((2 * LANES, 2 * LANES), BF16)
    planes = lambda *count: pltpu.VMEM(count + (N, LANES), F32)
    vmem, anywhere = pl.BlockSpec(memory_space=pltpu.VMEM), pl.BlockSpec(memory_space=pl.ANY)
    hbm = pl.BlockSpec(memory_space=pltpu.HBM)
    return pl.pallas_call(
        functools.partial(series_kernel, remote),
        out_shape=(
            jax.ShapeDtypeStruct((2,) + half, F32),
            jax.ShapeDtypeStruct((CH // 2, LANES), F32),
        ),
        in_specs=[pl.BlockSpec(memory_space=pltpu.SMEM)] + [vmem] + [hbm] * 7,
        out_specs=(anywhere, vmem),
        scratch_shapes=[
            pltpu.VMEM((2,) + half, F32),
            big(), pitch(), pitch(), big(), big(),
            pltpu.VMEM(half, F32),
            pltpu.VMEM((ROWS, N), F32),
            planes(), planes(2),
            square, square, square,
            pltpu.VMEM((2, ROWS, N), BF16),
            planes(3, 2), planes(3, 2), planes(), pltpu.VMEM((LANES, LANES), F32),
            planes(3), planes(3), planes(TERMS, 6),
            pltpu.VMEM((SRC, CH // 2, LANES), F32),
            pltpu.VMEM((SRC, CH // 2, LANES), F32),
            pltpu.SemaphoreType.DMA((TERMS, 6)),
            pltpu.SemaphoreType.DMA((TERMS, 6)),
            pltpu.SemaphoreType.DMA((SRC,)),
            pltpu.SemaphoreType.DMA((SRC,)),
            pltpu.SemaphoreType.DMA((SRC, 2)),
            pltpu.SemaphoreType.DMA((7,)),
        ],
        compiler_params=pltpu.CompilerParams(
            collective_id=0 if remote else None,
            has_side_effects=remote,
            vmem_limit_bytes=48 * 1024 * 1024,
        ),
    )(
        jnp.asarray(eig.astype(np.float32)),
        source,
        medium.reshape(ROWS, N),
        jnp.asarray(pair),
        jnp.asarray(wave),
        jnp.asarray(dft_table(-1.0)),
        jnp.asarray(dft_table(1.0)),
        jnp.asarray(dft_table(-1.0).T),
        adjoint.reshape(2, ROWS, N),
    )


def unpack_kernel(in_ref, total_ref, out_ref, grad_ref):
    for source, target in ((in_ref.at[0], out_ref.at[0]), (in_ref.at[1], out_ref.at[1]), (total_ref, grad_ref)):
        for n in range(source.shape[0] // N):
            pair = source[n * N : (n + 1) * N, :]
            for half in range(2):
                to = (2 * n + half) * N
                target[to : to + N, :] = pair[:, half * N : (half + 1) * N]


def unpack(packed, total, steps=4):
    rows, own = ROWS // steps, CH // steps
    return pl.pallas_call(
        unpack_kernel,
        grid=(steps,),
        out_shape=(jax.ShapeDtypeStruct((2, ROWS, N), F32), jax.ShapeDtypeStruct((CH, N), F32)),
        in_specs=[
            pl.BlockSpec((2, rows // 2, LANES), lambda i: (0, i, 0)),
            pl.BlockSpec((own // 2, LANES), lambda i: (i, 0)),
        ],
        out_specs=(
            pl.BlockSpec((2, rows, N), lambda i: (0, i, 0)),
            pl.BlockSpec((own, N), lambda i: (i, 0)),
        ),
        compiler_params=pltpu.CompilerParams(vmem_limit_bytes=12 * 1024 * 1024),
    )(packed, total)


def local(medium, source_cells, source_weights, adjoint):
    box = lax.axis_index("space").astype(jnp.int32).reshape(1)
    source = place(box, source_cells, source_weights)
    field, owned = unpack(*series(medium, source, adjoint))
    return field.reshape(2, 1, 1, N, N, N), owned.reshape(1, SLAB, N, N)


def solution(mesh):
    placed = (
        P("space", None, None, None),
        P("src", None),
        P(None, "src", None),
        P(None, "src", "space", None, None, None),
    )
    return jax.shard_map(
        local,
        mesh=mesh,
        in_specs=placed,
        out_specs=(P(None, "src", "space", None, None, None), P("space", "src", None, None)),
        check_vma=False,
    )
```

```python
import functools

import jax
import jax.numpy as jnp
import numpy as np
from jax import lax
from jax.experimental import pallas as pl
from jax.experimental.pallas import tpu as pltpu
from jax.sharding import PartitionSpec as P

N = 64
ROWS = N * N
LANES = 2 * N
TERMS = 2
BGX, BGY, BGZ = 2, 4, 4
SRC = 8
SLAB = N // SRC
CH = SLAB * N
DAMP = 0.25
PITCH = 68
BACK, BACKS = 512, 4
ITEM = 2048
MESH = pl.DeviceIdType.MESH
SLOTS = 256
F32, BF16 = jnp.float32, jnp.bfloat16


def split(values):
    high = values.astype(BF16)
    low = (values - high.astype(F32)).astype(BF16)
    return high, low


def dft_table(sign):
    k = np.arange(N)
    phase = 2.0 * np.pi / N * (k[:, None] * k[None, :] % N)
    c, s = np.cos(phase), sign * np.sin(phase)
    w = np.block([[c, s], [-s, c]]).astype(np.float32)
    high = w.astype(BF16)
    low = (w - high.astype(np.float32)).astype(BF16)
    half = np.concatenate([high, low], axis=1)
    return np.concatenate([half, half], axis=0)


def along_lanes(values, table):
    high, low = split(values)
    out = jnp.dot(jnp.concatenate([high, low], axis=1), table, preferred_element_type=F32)
    return out[:, :LANES] + out[:, LANES:]


def lower_half(rows):
    return lax.broadcasted_iota(jnp.int32, (rows, LANES), 1) < N


def trade(first, second):
    lower = lower_half(first.shape[0])
    crossed = pltpu.roll(jnp.where(lower, second, first), N, 1)
    return jnp.where(lower, first, crossed), jnp.where(lower, crossed, second)


def product_swapped(values, table, exchange=False):
    blocks = []
    for start in range(0, values.shape[0], 2 * LANES):
        high, low = split(values[start : start + 2 * LANES])
        both = jnp.concatenate([high, low], axis=1)
        out = lax.dot_general(table, both, (((1,), (1,)), ((), ())), preferred_element_type=F32)
        out = out[:LANES] + out[LANES:]
        for pair in range(out.shape[1] // LANES):
            turned = out[:, pair * LANES : (pair + 1) * LANES]
            first, second = turned[:N], turned[N:]
            blocks += trade(second, first) if exchange else trade(first, second)
    return jnp.concatenate(blocks, axis=0)


def staggered(count, stages):
    held = {}
    for turn in range(count + len(stages) - 1):
        for n in reversed(range(len(stages))):
            item = turn - n
            if 0 <= item < count:
                held[item] = stages[n](item, held.get(item))


def place_kernel(box_ref, cells_ref, weights_ref, out_ref, pos_ref, feat_ref):
    cells = cells_ref[...] - box_ref[0] * (N * N * N)
    inside = (cells >= 0) & (cells < N * N * N)
    mask = jnp.where(inside, 1.0, 0.0).astype(BF16)
    groups = cells.shape[0]
    i0 = lax.broadcasted_iota(jnp.int32, (128, 128), 0)
    i1 = lax.broadcasted_iota(jnp.int32, (128, 128), 1)
    upper = jnp.where(i0 < i1, 1.0, 0.0).astype(BF16)
    within = jnp.dot(mask, upper, preferred_element_type=F32)
    totals = jnp.dot(mask, jnp.ones((128, 128), BF16), preferred_element_type=F32)
    j0 = lax.broadcasted_iota(jnp.int32, (groups, groups), 0)
    j1 = lax.broadcasted_iota(jnp.int32, (groups, groups), 1)
    before = jnp.where(j1 < j0, 1.0, 0.0).astype(BF16)
    offset = jnp.dot(before, totals.astype(BF16), preferred_element_type=F32)
    pos_ref[...] = jnp.where(inside, (within + offset).astype(jnp.int32), -1)
    count = jnp.sum(jnp.where(inside, 1, 0))
    safe = jnp.where(inside, cells, 0)
    rh, rl = split(weights_ref[0])
    ih, il = split(weights_ref[1])
    rows = (
        (safe >> 13).astype(F32),
        ((safe >> 6) & (N - 1)).astype(F32),
        (((safe >> 12) & 1) * N + (safe & (N - 1))).astype(F32),
        rh.astype(F32),
        rl.astype(F32),
        ih.astype(F32),
        il.astype(F32),
    )
    for n, row in enumerate(rows):
        feat_ref[n] = row

    def chunk(step, carry):
        slot = lax.broadcasted_iota(jnp.int32, (SLOTS, 128), 0) + step * SLOTS
        sub = lax.broadcasted_iota(jnp.int32, (16, 128), 0)
        hots, feats = [], []
        for g in range(groups):
            hots.append(jnp.where(pos_ref[g : g + 1, :] == slot, 1.0, 0.0).astype(BF16))
            f = jnp.zeros((16, 128), F32)
            for n in range(len(rows)):
                f = jnp.where(sub == n, feat_ref[n, g : g + 1, :], f)
            feats.append(f.astype(BF16))
        hot = jnp.concatenate(hots, axis=1)
        feat = jnp.concatenate(feats, axis=1)
        nt = (((1,), (1,)), ((), ()))
        by_lane = lax.dot_general(feat, hot, nt, preferred_element_type=F32)
        by_row = by_lane.T
        used = lax.broadcasted_iota(jnp.int32, (1, SLOTS), 1) + step * SLOTS < count
        plane = (by_lane[0:1] * N + by_lane[1:2]).astype(jnp.int32)
        plane = jnp.where(used, plane, -1)
        lane = lax.broadcasted_iota(jnp.int32, (SLOTS, LANES), 1)
        hit = lane == by_row[:, 2:3].astype(jnp.int32)
        spread = [jnp.where(hit, by_row[:, n : n + 1], 0.0) for n in range(3, 7)]
        spread = jnp.concatenate(spread, axis=1).astype(BF16)

        def rows_of(block, inner):
            start = pl.multiple_of(block * 256, 256)
            at = lax.broadcasted_iota(jnp.int32, (256, SLOTS), 0) + start
            pick = jnp.where(at == plane, 1.0, 0.0).astype(BF16)
            got = jnp.dot(pick, spread, preferred_element_type=F32)
            for part in range(2):
                one = got[:, 2 * part * LANES : (2 * part + 1) * LANES]
                one = one + got[:, (2 * part + 1) * LANES : (2 * part + 2) * LANES]
                old = out_ref[part, pl.ds(start, 256), :]
                out_ref[part, pl.ds(start, 256), :] = jnp.where(step > 0, old, 0.0) + one
            return inner

        return lax.fori_loop(0, ROWS // 512, rows_of, carry)

    lax.fori_loop(0, jnp.maximum(1, (count + SLOTS - 1) // SLOTS), chunk, 0)


def place(box, cells, weights):
    groups = cells.shape[-1] // 128
    return pl.pallas_call(
        place_kernel,
        out_shape=jax.ShapeDtypeStruct((2, ROWS // 2, LANES), F32),
        in_specs=[pl.BlockSpec(memory_space=pltpu.SMEM)]
        + [pl.BlockSpec(memory_space=pltpu.VMEM)] * 2,
        out_specs=pl.BlockSpec(memory_space=pltpu.VMEM),
        scratch_shapes=[pltpu.VMEM((groups, 128), jnp.int32), pltpu.VMEM((8, groups, 128), F32)],
        compiler_params=pltpu.CompilerParams(vmem_limit_bytes=12 * 1024 * 1024),
    )(box, cells.reshape(groups, 128), weights.reshape(2, groups, 128))


def series_kernel(
    remote,
    eig_ref, source_ref, medium_hbm, pair_hbm, wave_hbm, fwd_hbm, inv_hbm, turn_hbm, adjoint_hbm,
    out_hbm, grad_ref,
    packed, drive, one, two, kre, kim, pot, medium, pair_ref, wave_ref, fwd_ref, inv_ref, turn_ref, adjoint,
    faces, ratios, ends, turns, sums, zcor, recv, gsend, grecv,
    send_sem, recv_sem, gsend_sem, grecv_sem, out_sem, in_sem,
):
    fre, fim = packed.at[0], packed.at[1]
    loads = [
        pltpu.make_async_copy(there, here, in_sem.at[n])
        for n, (there, here) in enumerate(
            (
                (pair_hbm, pair_ref),
                (medium_hbm, medium),
                (wave_hbm, wave_ref),
                (fwd_hbm, fwd_ref),
                (inv_hbm, inv_ref),
                (turn_hbm, turn_ref),
                (adjoint_hbm, adjoint),
            )
        )
    ]
    for load in loads:
        load.start()
    if remote:
        space, me = lax.axis_index("space"), lax.axis_index("src")
        bx, by, bz = space // (BGY * BGZ), space // BGZ % BGY, space % BGZ
        below = (
            lax.rem(bx + BGX - 1, BGX) * (BGY * BGZ) + by * BGZ + bz,
            bx * (BGY * BGZ) + lax.rem(by + BGY - 1, BGY) * BGZ + bz,
            bx * (BGY * BGZ) + by * BGZ + lax.rem(bz + BGZ - 1, BGZ),
        )
        above = (
            lax.rem(bx + 1, BGX) * (BGY * BGZ) + by * BGZ + bz,
            bx * (BGY * BGZ) + lax.rem(by + 1, BGY) * BGZ + bz,
            bx * (BGY * BGZ) + by * BGZ + lax.rem(bz + 1, BGZ),
        )
        has_below = [(v > 0).astype(F32) for v in (bx, by, bz)]
        has_above = [(v < e - 1).astype(F32) for v, e in ((bx, BGX), (by, BGY), (bz, BGZ))]
        barrier = pltpu.get_barrier_semaphore()
        for d in range(3):
            for other in (below[d], above[d]):
                pl.semaphore_signal(barrier, 1, device_id={"space": other}, device_id_type=MESH)
        for k in range(1, SRC):
            pl.semaphore_signal(
                barrier, 1, device_id={"src": lax.rem(me + k, SRC)}, device_id_type=MESH
            )
    else:
        me = 0

    low = lower_half(N)

    def table(z, carry):
        shifted = pair_ref[...] + eig_ref[z]
        scale = 1.0 / ((shifted * shifted + DAMP * DAMP) * float(N**3))
        real, imag = shifted * scale, jnp.where(low, -DAMP, DAMP) * scale
        for same in (z, lax.rem(N - z, N)):
            rows = pl.ds(pl.multiple_of(same * N, N), N)
            kre[rows, :] = real
            kim[rows, :] = imag
        return carry

    loads[0].wait()
    lax.fori_loop(0, N // 2 + 1, table, 0)

    def half_rows(pair):
        return pl.ds(pl.multiple_of(pair * N, N), N)

    def plane_rows(pair, half):
        return pl.ds(pl.multiple_of((2 * pair + half) * N, N), N)

    def pitched(pair, half):
        return pl.ds((2 * pair + half) * PITCH, N)

    def put_drive(pair, re, im):
        for half, rows in enumerate(trade(re, im)):
            drive[plane_rows(pair, half), :] = rows

    def begin(pair, carry):
        rows = half_rows(pair)
        fre[rows, :] = jnp.zeros((N, LANES), F32)
        fim[rows, :] = jnp.zeros((N, LANES), F32)
        put_drive(pair, source_ref[0, rows, :], source_ref[1, rows, :])
        return carry

    lax.fori_loop(0, N // 2, begin, 0)
    faces[...] = jnp.zeros_like(faces)
    zcor[...] = jnp.zeros_like(zcor)
    lane = lax.broadcasted_iota(jnp.int32, (N, LANES), 1)

    loads[1].wait()

    def potential(pair, carry):
        both = [medium[plane_rows(pair, half), :] - 1.0 for half in range(2)]
        both = jnp.concatenate(both, axis=1)
        pot[half_rows(pair), :] = both
        moved = pltpu.roll(both, 1 + 2 * pair, 1)
        ends[...] = jnp.where((lane % N) // 2 == pair, moved, ends[...])
        return carry

    lax.fori_loop(0, N // 2, potential, 0)
    turns[...] = jnp.concatenate([ends[...], ends[...]], axis=0).T
    half = N // 2
    for face, (even, odd) in enumerate(((1, N + 1), (N, 0))):
        ratios[2, face, pl.ds(0, half, stride=2), :] = turns[pl.ds(even, half, stride=2), :]
        ratios[2, face, pl.ds(1, half, stride=2), :] = turns[pl.ds(odd, half, stride=2), :]
    for d, planes in (
        (0, (pl.ds(0, N), pl.ds(ROWS - N, N))),
        (1, (pl.ds(0, N, stride=N), pl.ds(N - 1, N, stride=N))),
    ):
        for face in range(2):
            plane = medium[planes[face], :] - 1.0
            ratios[d, face] = jnp.concatenate([plane, plane], axis=1)
    ratios[...] = jnp.where(lower_half(N), -1.0 / DAMP, 1.0 / DAMP) * ratios[...]

    for load in loads[2:6]:
        load.wait()

    def forward():
        def load(p, _):
            return product_swapped(drive[pl.ds(p * ITEM, ITEM), :], turn_ref[...])

        def store(p, values):
            for n in range(ITEM // N):
                x = p * (ITEM // N) + n
                extra = (
                    zcor[0, pl.ds(x, 1), :]
                    + wave_ref[0] * zcor[1, pl.ds(x, 1), :]
                    + wave_ref[1] * zcor[2, pl.ds(x, 1), :]
                )
                to = pl.ds(x * PITCH, N)
                one[to, :] = values[n * N : (n + 1) * N] + extra

        staggered(ROWS // ITEM, (load, store))

    def middle():
        def strided(p, n):
            return pl.ds(p * (ITEM // N) + n, N, stride=PITCH)

        def load(p, _):
            values = [one[strided(p, n), :] for n in range(ITEM // N)]
            return product_swapped(jnp.concatenate(values, axis=0), turn_ref[...])

        def product(p, values):
            values = along_lanes(values, fwd_ref[...])
            rows = pl.ds(p * ITEM, ITEM)
            return kre[rows, :] * pltpu.roll(values, N, 1) - kim[rows, :] * values

        def store(p, values):
            values = product_swapped(values, turn_ref[...])
            for n in range(ITEM // N):
                two[strided(p, n), :] = values[n * N : (n + 1) * N]

        staggered(ROWS // ITEM, (load, product, store))

    def back_swap(item, ends):
        planes = []
        for n in range(BACK // N):
            x = item * (BACK // N) + n
            plane = two[pl.ds(x * PITCH, N), :]
            planes.append(plane)
            if ends:
                sums[0, pl.ds(x, 1), :] = jnp.sum(plane, axis=0, keepdims=True)
                for part in range(2):
                    waved = jnp.sum(wave_ref[part] * plane, axis=0, keepdims=True)
                    sums[1 + part, pl.ds(x, 1), :] = waved
        return product_swapped(jnp.concatenate(planes, axis=0), turn_ref[...], exchange=True)

    def back_rows(item):
        return pl.ds(pl.multiple_of(item * BACK, BACK), BACK)

    def updated(pair, even, odd):
        rows = half_rows(pair)
        gre, gim = trade(even, odd)
        ratio = pot[rows, :] * (1.0 / DAMP)
        return gre + ratio * (fim[rows, :] - gim), gim - ratio * (fre[rows, :] - gre)

    def finish_term(step):
        def swap_pass(i, inner):
            for p in range(BACKS):
                one[back_rows(i * BACKS + p), :] = back_swap(i * BACKS + p, True)
            return inner

        lax.fori_loop(0, ROWS // BACK // BACKS, swap_pass, 0)

        turned = lambda values: pltpu.roll(values, N, 1)
        edges = (
            (pl.ds(0, N), pl.ds(ROWS - N, N)),
            (pl.ds(0, N, stride=N), pl.ds(N - 1, N, stride=N)),
        )
        rows = [one[edges[d][face], :] for d in range(2) for face in range(2)]
        rows = along_lanes(jnp.concatenate(rows, axis=0), inv_ref[...])
        total = along_lanes(sums[...].reshape(3 * N, LANES), fwd_ref[...]).reshape(3, N, LANES)
        greens = (
            (rows[:N], rows[N : 2 * N]),
            (rows[2 * N : 3 * N], rows[3 * N :]),
            (turned(total[0]), turned(total[1]) + jnp.where(low, total[2], -total[2])),
        )
        if remote:

            @pl.when(step == 0)
            def _():
                pl.semaphore_wait(barrier, 6 + SRC - 1)

        copies = {}
        for d in (1, 2, 0):
            for face in range(2):
                green = greens[d][face]
                faces[d, face] = green - ratios[d, face] * turned(faces[d, face] - green)
            if remote:
                for side, other in ((1, above[d]), (0, below[d])):
                    slot = 1 - side
                    copies[d, slot] = pltpu.make_async_remote_copy(
                        src_ref=faces.at[d, side],
                        dst_ref=recv.at[step, 2 * d + slot],
                        send_sem=send_sem.at[step, 2 * d + slot],
                        recv_sem=recv_sem.at[step, 2 * d + slot],
                        device_id={"space": other},
                        device_id_type=MESH,
                    )
                    copies[d, slot].start()

        def z_pass(i, inner):
            def load(p, _):
                return along_lanes(one[back_rows(i * BACKS + p), :], inv_ref[...])

            def update(p, values):
                for n in range(BACK // LANES):
                    pair = (i * BACKS + p) * (BACK // LANES) + n
                    rows = half_rows(pair)
                    re, im = updated(pair, *(values[(2 * n + h) * N : (2 * n + h + 1) * N] for h in range(2)))
                    fre[rows, :] = re
                    fim[rows, :] = im
                    put_drive(
                        pair,
                        pot[rows, :] * re + DAMP * im + source_ref[0, rows, :],
                        pot[rows, :] * im - DAMP * re + source_ref[1, rows, :],
                    )

            staggered(BACKS, (load, update))
            return inner

        lax.fori_loop(0, ROWS // BACK // BACKS, z_pass, 0)

        def difference(d, slot):
            if not remote:
                return -faces[d, 1 - slot]
            copies[d, slot].wait_recv()
            there = (has_below if slot == 0 else has_above)[d]
            return there * recv[step, 2 * d + slot] - faces[d, 1 - slot]

        for d in (0, 1):
            for slot in range(2):
                drive[edges[d][slot], :] = drive[edges[d][slot], :] + difference(d, slot)
        zcor[0] = difference(2, 0)
        upper_end = difference(2, 1)
        zcor[1] = upper_end
        zcor[2] = jnp.where(low, -1.0, 1.0) * turned(upper_end)
        for copy in copies.values():
            copy.wait_send()

    def grad_copy(owner, slot):
        return pltpu.make_async_remote_copy(
            src_ref=gsend.at[owner],
            dst_ref=grecv.at[slot],
            send_sem=gsend_sem.at[owner],
            recv_sem=grecv_sem.at[slot],
            device_id={"src": owner},
            device_id_type=MESH,
        )

    def out_copy(i, part):
        rows = pl.ds(pl.multiple_of(i * (CH // 2), CH // 2), CH // 2)
        return pltpu.make_async_copy(
            packed.at[part, rows], out_hbm.at[part, rows], out_sem.at[i, part]
        )

    def last_pass(k, carry):
        i = lax.rem(me // 2 + 2 + lax.rem(k, 4) - k // 4, 4) * 2 + lax.rem(me + 1 - k // 4, 2)
        items = CH // BACK

        def load(p, _):
            return back_swap(i * items + p, False)

        def update(p, values):
            values = along_lanes(values, inv_ref[...])
            for n in range(BACK // LANES):
                pair = (i * items + p) * (BACK // LANES) + n
                new = updated(pair, *(values[(2 * n + h) * N : (2 * n + h + 1) * N] for h in range(2)))
                fre[half_rows(pair), :] = new[0]
                fim[half_rows(pair), :] = new[1]
                terms = []
                for part in range(2):
                    sides = [adjoint[part, plane_rows(pair, half), :].astype(F32) for half in range(2)]
                    terms.append(jnp.concatenate(sides, axis=1) * new[part])
                to = (p * (BACK // LANES) + n) * N
                gsend[i, to : to + N, :] = terms[0] - terms[1]

        staggered(items, (load, update))
        for part in range(2):
            out_copy(i, part).start()
        if remote:

            @pl.when(k < SRC - 1)
            def _():
                grad_copy(i, me).start()

        return carry

    def finish():
        loads[6].wait()
        lax.fori_loop(0, SRC, last_pass, 0)
        total = gsend[me]
        if remote:
            for k in range(1, SRC):
                other = lax.rem(me + k, SRC)
                grad_copy(other, other).wait_recv()
                total = total + grecv[other]
        grad_ref[...] = total
        if remote:
            for k in range(1, SRC):
                grad_copy(lax.rem(me + k, SRC), me).wait_send()
        for i in range(SRC):
            for part in range(2):
                out_copy(i, part).wait()

    def term(step, carry):
        forward()
        middle()
        pl.when(step < TERMS)(lambda: finish_term(step))
        pl.when(step == TERMS)(finish)
        return carry

    lax.fori_loop(0, TERMS + 1, term, 0)


def series(medium, source, adjoint, remote=True):
    k = np.arange(N)
    eig = 2.0 - 2.0 * np.cos(2.0 * np.pi / N * k)
    pair = (eig[:, None] + np.tile(eig, 2)[None, :] - 1.0).astype(np.float32)
    wave = np.stack([np.cos(2.0 * np.pi / N * k), np.sin(2.0 * np.pi / N * k)])
    wave = np.repeat(wave[:, :, None], LANES, axis=2).astype(np.float32)
    half = (ROWS // 2, LANES)
    big = lambda: pltpu.VMEM((ROWS, LANES), F32)
    pitch = lambda: pltpu.VMEM((N * PITCH, LANES), F32)
    square = pltpu.VMEM((2 * LANES, 2 * LANES), BF16)
    planes = lambda *count: pltpu.VMEM(count + (N, LANES), F32)
    vmem, anywhere = pl.BlockSpec(memory_space=pltpu.VMEM), pl.BlockSpec(memory_space=pl.ANY)
    hbm = pl.BlockSpec(memory_space=pltpu.HBM)
    return pl.pallas_call(
        functools.partial(series_kernel, remote),
        out_shape=(
            jax.ShapeDtypeStruct((2,) + half, F32),
            jax.ShapeDtypeStruct((CH // 2, LANES), F32),
        ),
        in_specs=[pl.BlockSpec(memory_space=pltpu.SMEM)] + [vmem] + [hbm] * 7,
        out_specs=(anywhere, vmem),
        scratch_shapes=[
            pltpu.VMEM((2,) + half, F32),
            big(), pitch(), pitch(), big(), big(),
            pltpu.VMEM(half, F32),
            pltpu.VMEM((ROWS, N), F32),
            planes(), planes(2),
            square, square, square,
            pltpu.VMEM((2, ROWS, N), BF16),
            planes(3, 2), planes(3, 2), planes(), pltpu.VMEM((LANES, LANES), F32),
            planes(3), planes(3), planes(TERMS, 6),
            pltpu.VMEM((SRC, CH // 2, LANES), F32),
            pltpu.VMEM((SRC, CH // 2, LANES), F32),
            pltpu.SemaphoreType.DMA((TERMS, 6)),
            pltpu.SemaphoreType.DMA((TERMS, 6)),
            pltpu.SemaphoreType.DMA((SRC,)),
            pltpu.SemaphoreType.DMA((SRC,)),
            pltpu.SemaphoreType.DMA((SRC, 2)),
            pltpu.SemaphoreType.DMA((7,)),
        ],
        compiler_params=pltpu.CompilerParams(
            collective_id=0 if remote else None,
            has_side_effects=remote,
            vmem_limit_bytes=48 * 1024 * 1024,
        ),
    )(
        jnp.asarray(eig.astype(np.float32)),
        source,
        medium.reshape(ROWS, N),
        jnp.asarray(pair),
        jnp.asarray(wave),
        jnp.asarray(dft_table(-1.0)),
        jnp.asarray(dft_table(1.0)),
        jnp.asarray(dft_table(-1.0).T),
        adjoint.reshape(2, ROWS, N),
    )


def unpack_kernel(in_ref, total_ref, out_ref, grad_ref):
    for source, target in ((in_ref.at[0], out_ref.at[0]), (in_ref.at[1], out_ref.at[1]), (total_ref, grad_ref)):
        for n in range(source.shape[0] // N):
            pair = source[n * N : (n + 1) * N, :]
            for half in range(2):
                to = (2 * n + half) * N
                target[to : to + N, :] = pair[:, half * N : (half + 1) * N]


def unpack(packed, total, steps=4):
    rows, own = ROWS // steps, CH // steps
    return pl.pallas_call(
        unpack_kernel,
        grid=(steps,),
        out_shape=(jax.ShapeDtypeStruct((2, ROWS, N), F32), jax.ShapeDtypeStruct((CH, N), F32)),
        in_specs=[
            pl.BlockSpec((2, rows // 2, LANES), lambda i: (0, i, 0)),
            pl.BlockSpec((own // 2, LANES), lambda i: (i, 0)),
        ],
        out_specs=(
            pl.BlockSpec((2, rows, N), lambda i: (0, i, 0)),
            pl.BlockSpec((own, N), lambda i: (i, 0)),
        ),
        compiler_params=pltpu.CompilerParams(vmem_limit_bytes=12 * 1024 * 1024),
    )(packed, total)


def local(medium, source_cells, source_weights, adjoint):
    box = lax.axis_index("space").astype(jnp.int32).reshape(1)
    source = place(box, source_cells, source_weights)
    field, owned = unpack(*series(medium, source, adjoint))
    return field.reshape(2, 1, 1, N, N, N), owned.reshape(1, SLAB, N, N)


def solution(mesh):
    placed = (
        P("space", None, None, None),
        P("src", None),
        P(None, "src", None),
        P(None, "src", "space", None, None, None),
    )
    return jax.shard_map(
        local,
        mesh=mesh,
        in_specs=placed,
        out_specs=(P(None, "src", "space", None, None, None), P("space", "src", None, None)),
        check_vma=False,
    )
```
